32 devices in a mesh: pts: 4 (over y, core), grid: 8 (over z, x).
Axes of the slice: x: 2, y: 2, z: 4, core: 2. Of those that a mesh axis runs over, the one named last changes fastest.
Arguments:
- features: bfloat16 [32, 524288], P(None, ('pts', 'grid')), may hold values from -6 to 6
- w_in: bfloat16 [32, 64], replicated, may hold values from -1 to 1
- w_mid: bfloat16 [64, 64], replicated, may hold values from -0.75 to 0.75
- w_conv: bfloat16 [2, 3, 3, 3, 64, 64], replicated, may hold values from -0.15625 to 0.15625
- point_frac: float32 [3, 524288], P(None, ('pts', 'grid')), may hold values from 0 to 1
- point_base: int32 [3, 524288], P(None, ('pts', 'grid')), may hold values from 0 to 6, as said below
- slot_dest: int32 [2048], P(('pts', 'grid')), may hold values from 0 to 7, as said below
- slot_tile_block: int32 [2048], P(('pts', 'grid')), may hold values from 0 to 63
- slot_count: int32 [2048], P(('pts', 'grid')), may hold values from 1 to 256, as said below
Outputs:
- point_out: bfloat16 [64, 524288], P(None, ('pts', 'grid'))
The draws below stay inside these ranges and needn't reach their ends.
Inputs may be any that keep to these rules, and one draw needn't show every extreme that they name: `point_base`: the three rows give base cells along the first, second and third dimension; the first two rows lie in 0 .. 2 and the third in 0 .. 6, so all eight corners of a point lie in its block. `slot_dest`: among the 64 slots of one device at most 16 name the same value; on every device one value is named by exactly 16 slots, the same value on all devices of one index along pts. `slot_count`: every device has a slot with exactly 256 live points.
All inputs are finite; a program needn't handle non-finite values.
Results may differ from the reference program's by a relative error of at most 0.0035.
The reference program's roundings to bfloat16 on the way count: a program that leaves them out, or rounds other values in their place, can miss the bound.
Values may be sent and summed in bfloat16 or wider, within the bound.
A program may use at most 128 MiB of HBM per device.

```python
import jax
import jax.numpy as jnp
from jax import lax

CIN = 32
HID = 64
GZ = 8
BLOCK_EDGE_CELLS = 4
LAYERS = 2
TX = 32
TY = 32
DEVICE_SLOTS = 64
CAP = 256
CAPB = 16
NXG = 256
NYG = 128
SLOT_COUNT_ALL = 2048
NPT = 524288
TILE_BLOCK_COUNT = 64
N_PTS = 4
N_GRID = 8


def draw_point_base(key, part):
    first_two = jax.random.randint(jax.random.fold_in(key, 1), (2, NPT), 0, BLOCK_EDGE_CELLS - 1)
    third_row = jax.random.randint(jax.random.fold_in(key, 2), (1, NPT), 0, GZ - 1)
    return jnp.concatenate([first_two, third_row], axis=0).astype(jnp.int32)


def draw_slot_dest(key, part):
    devices = N_PTS * N_GRID
    hot_row = jax.random.randint(jax.random.fold_in(key, 3), (N_PTS,), 0, N_GRID)
    hot_owner = jnp.repeat(hot_row, N_GRID)
    spare_total = (N_GRID - 1) * CAPB

    def one_device(device_key, owner):
        pool_values = jnp.arange(spare_total, dtype=jnp.int32) // CAPB
        pool_values = pool_values + (pool_values >= owner).astype(jnp.int32)
        picked = jax.random.permutation(jax.random.fold_in(device_key, 1), pool_values)[:DEVICE_SLOTS - CAPB]
        whole_list = jnp.concatenate([jnp.full((CAPB,), owner, jnp.int32), picked.astype(jnp.int32)])
        return jax.random.permutation(jax.random.fold_in(device_key, 2), whole_list)
    device_keys = jax.random.split(jax.random.fold_in(key, 4), devices)
    return jax.vmap(one_device)(device_keys, hot_owner).reshape(-1).astype(jnp.int32)


def draw_slot_count(key, part):
    devices = N_PTS * N_GRID
    counts = jax.random.randint(jax.random.fold_in(key, 5), (devices, DEVICE_SLOTS), 1, CAP + 1)
    full_at = jax.random.randint(jax.random.fold_in(key, 6), (devices, 1), 0, DEVICE_SLOTS)
    counts = jnp.where(jnp.arange(DEVICE_SLOTS, dtype=jnp.int32)[None, :] == full_at, CAP, counts)
    return counts.reshape(-1).astype(jnp.int32)


def set_ends(result, own_key, low, high):
    longest = result.shape.index(max(result.shape))
    spots = []
    for shift in (0, 1):
        where = [jax.random.randint(jax.random.fold_in(own_key, axis), (), 0, length) for axis, length in enumerate(result.shape)]
        where[longest] = (where[longest] + shift) % result.shape[longest]
        spots.append(tuple(where))
    return result.at[spots[0]].set(low).at[spots[1]].set(high)


def block_levels(stream_key, dims, cuts, smallest, top_value):
    level, own = 1.0, jax.random.fold_in(stream_key, 6)
    for position, shards_of in cuts:
        steps = jnp.exp(jax.random.uniform(jax.random.fold_in(own, position), (shards_of,), jnp.float32, smallest / len(cuts), top_value / len(cuts)))
        level = level * jnp.repeat(steps, dims[position] // shards_of).reshape([-1 if axis == position else 1 for axis in range(len(dims))])
    return level


def gaussian(key, extent, scale, limit, cuts=(), kind=jnp.bfloat16):
    entries = jax.random.normal(key, extent, jnp.float32) * scale
    if len(cuts) > 0:
        entries = block_levels(key, extent, cuts, -0.22, 0.18) * entries
    return jnp.clip(entries, min=-limit, max=limit).astype(kind)


def setup_inputs(seed: int = 0) -> dict:
    arg_keys = jax.random.split(jax.random.key(seed), 10)
    features = gaussian(arg_keys[0], (CIN, NPT), 1.0, 6.0, ((1, 32),))
    w_in = gaussian(arg_keys[1], (CIN, HID), CIN ** -0.5, 1.0)
    w_mid = gaussian(arg_keys[2], (HID, HID), HID ** -0.5, 0.75)
    w_conv = gaussian(arg_keys[3], (LAYERS, 3, 3, 3, HID, HID), (27 * HID) ** -0.5, 0.15625)
    point_frac = jnp.clip(1.0 * jax.random.uniform(arg_keys[4], (3, NPT), jnp.float32) ** block_levels(arg_keys[4], (3, NPT), ((1, 32),), -0.2, 0.2), 0.0, 1.0)
    point_base = draw_point_base(jax.random.fold_in(arg_keys[9], 71), 0)
    slot_dest = draw_slot_dest(jax.random.fold_in(arg_keys[9], 71), 0)
    slot_tile_block = set_ends(jax.random.randint(arg_keys[7], (SLOT_COUNT_ALL,), 0, TILE_BLOCK_COUNT), jax.random.fold_in(arg_keys[7], 1), 0, TILE_BLOCK_COUNT - 1).astype(jnp.int32)
    slot_count = draw_slot_count(jax.random.fold_in(arg_keys[9], 71), 0)
    return {"features": features, "w_in": w_in, "w_mid": w_mid, "w_conv": w_conv, "point_frac": point_frac, "point_base": point_base, "slot_dest": slot_dest, "slot_tile_block": slot_tile_block, "slot_count": slot_count}


def axis_weights(offset, corner, length):
    positions = jnp.arange(length, dtype=jnp.int32)[:, None, None]
    below_part = jnp.where(positions == corner[None], 1.0 - offset[None], 0.0)
    above_part = jnp.where(positions == corner[None] + 1, offset[None], 0.0)
    return below_part + above_part


def trilinear(offsets, corners, counts, block_edge, grid_depth):
    slot_width = offsets.shape[2]
    live_mask = (jnp.arange(slot_width, dtype=jnp.int32)[None, :] < counts[:, None]).astype(jnp.float32)
    along_x = axis_weights(offsets[0], corners[0], block_edge)
    along_y = axis_weights(offsets[1], corners[1], block_edge)
    along_z = axis_weights(offsets[2], corners[2], grid_depth)
    corner_weights = along_x[:, None, None] * along_y[None, :, None] * along_z[None, None, :] * live_mask
    return corner_weights.reshape(block_edge * block_edge, grid_depth, offsets.shape[1], slot_width).astype(jnp.bfloat16)


def point_layer(weight, inputs):
    mixed_sum = jnp.dot(weight.T, inputs, preferred_element_type=jnp.float32)
    return jax.nn.silu(mixed_sum).astype(jnp.bfloat16)


def banded_weights(kernel, grid_depth):
    depth_range = jnp.arange(grid_depth, dtype=jnp.int32)
    shifts = (depth_range[None, :, None] == depth_range[None, None, :] + jnp.arange(3, dtype=jnp.int32)[:, None, None] - 1).astype(jnp.float32)
    banded = jnp.einsum("kab,xykij->xyaibj", shifts, kernel.astype(jnp.float32))
    return banded.astype(jnp.bfloat16).reshape(3, 3, grid_depth * kernel.shape[3], grid_depth * kernel.shape[4])


def reference(features, w_in, w_mid, w_conv, point_frac, point_base, slot_dest, slot_tile_block, slot_count):
    devices = N_PTS * N_GRID
    per_device = DEVICE_SLOTS * CAP
    every_channel = GZ * HID
    feats_dev = features.reshape(CIN, devices, per_device).transpose(1, 0, 2)
    frac_dev = point_frac.reshape(3, devices, DEVICE_SLOTS, CAP).transpose(1, 0, 2, 3)
    base_dev = point_base.reshape(3, devices, DEVICE_SLOTS, CAP).transpose(1, 0, 2, 3)
    count_dev = slot_count.reshape(devices, DEVICE_SLOTS)

    def local_part(feats, offsets, corners, counts):
        hidden_two = point_layer(w_mid, point_layer(w_in, feats)).reshape(HID, DEVICE_SLOTS, CAP)
        weights = trilinear(offsets, corners, counts, BLOCK_EDGE_CELLS, GZ)
        return hidden_two, weights

    def splat_part(packed):
        hidden_two, weights = local_part(*packed)
        sums = jnp.einsum("czsp,hsp->sczh", weights.astype(jnp.float32), hidden_two.astype(jnp.float32))
        return sums.astype(jnp.bfloat16).reshape(DEVICE_SLOTS, BLOCK_EDGE_CELLS * BLOCK_EDGE_CELLS * every_channel)

    partial_sums = lax.map(splat_part, (feats_dev, frac_dev, base_dev, count_dev))
    nbx_local = TX // BLOCK_EDGE_CELLS
    nby_local = TY // BLOCK_EDGE_CELLS
    blocks_along_first = nbx_local * N_GRID
    blocks_along_second = nby_local * N_PTS
    slot_owner_device = jnp.arange(SLOT_COUNT_ALL, dtype=jnp.int32) // DEVICE_SLOTS
    row_pts = slot_owner_device // N_GRID
    block_x = slot_dest * nbx_local + slot_tile_block // nby_local
    block_y = row_pts * nby_local + slot_tile_block % nby_local
    block_number = (block_x * blocks_along_second + block_y).astype(jnp.int32)
    summed_blocks = jax.ops.segment_sum(partial_sums.reshape(SLOT_COUNT_ALL, BLOCK_EDGE_CELLS * BLOCK_EDGE_CELLS * every_channel).astype(jnp.float32), block_number, num_segments=blocks_along_first * blocks_along_second)
    grid = summed_blocks.astype(jnp.bfloat16).reshape(blocks_along_first, blocks_along_second, BLOCK_EDGE_CELLS, BLOCK_EDGE_CELLS, every_channel)
    grid = grid.transpose(0, 2, 1, 3, 4).reshape(NXG, NYG, every_channel)
    for layer_index in range(LAYERS):
        banded = banded_weights(w_conv[layer_index], GZ).astype(jnp.float32)
        padded = jnp.pad(grid, ((1, 1), (1, 1), (0, 0))).astype(jnp.float32)
        total_sum = jnp.zeros((NXG, NYG, every_channel), jnp.float32)
        for shift_x in range(3):
            for shift_y in range(3):
                window = padded[shift_x:shift_x + NXG, shift_y:shift_y + NYG]
                total_sum = total_sum + jnp.einsum("xyi,ij->xyj", window, banded[shift_x, shift_y])
        grid = jax.nn.silu(total_sum).astype(jnp.bfloat16)
    blocks = grid.reshape(blocks_along_first, BLOCK_EDGE_CELLS, blocks_along_second, BLOCK_EDGE_CELLS, every_channel).transpose(0, 2, 1, 3, 4)
    blocks = blocks.reshape(blocks_along_first * blocks_along_second, BLOCK_EDGE_CELLS * BLOCK_EDGE_CELLS, every_channel)
    slot_cells = blocks[block_number].reshape(devices, DEVICE_SLOTS, BLOCK_EDGE_CELLS * BLOCK_EDGE_CELLS, GZ, HID)

    def finish_part(packed):
        feats, offsets, corners, counts, cells = packed
        hidden_two, weights = local_part(feats, offsets, corners, counts)
        interp = jnp.einsum("czsp,sczh->hsp", weights.astype(jnp.float32), cells.astype(jnp.float32)).astype(jnp.bfloat16)
        point_out = (hidden_two.astype(jnp.float32) + interp.astype(jnp.float32)).astype(jnp.bfloat16)
        return point_out.reshape(HID, per_device)

    results = lax.map(finish_part, (feats_dev, frac_dev, base_dev, count_dev, slot_cells))
    return results.transpose(1, 0, 2).reshape(HID, NPT)
```

```python
import functools

import jax
import jax.numpy as jnp
import numpy as np
from jax import lax
from jax.experimental import pallas as pl
from jax.experimental.pallas import tpu as pltpu
from jax.sharding import PartitionSpec as P

GZ = 8
BLOCK_EDGE_CELLS = 4
TX = 32
TY = 32
ID_LANES = 128
MESH = pl.DeviceIdType.MESH
DIRECTIONS = ((1, 0), (-1, 0), (0, 1), (0, -1), (1, 1), (1, -1), (-1, 1), (-1, -1))


def point_layer(weight, inputs):
    mixed_sum = lax.dot_general(
        weight, inputs, (((0,), (0,)), ((), ())), preferred_element_type=jnp.float32
    )
    return jax.nn.silu(mixed_sum).astype(jnp.bfloat16)


def axis_weights(offset, corner, length):
    positions = jnp.arange(length, dtype=jnp.int32)[:, None, None]
    below_part = jnp.where(positions == corner[None], 1.0 - offset[None], 0.0)
    above_part = jnp.where(positions == corner[None] + 1, offset[None], 0.0)
    return below_part + above_part


def trilinear(offsets, corners, counts, block_edge, grid_depth):
    slot_width = offsets.shape[2]
    live_mask = (jnp.arange(slot_width, dtype=jnp.int32)[None, :] < counts[:, None]).astype(
        jnp.float32
    )
    along_x = axis_weights(offsets[0], corners[0], block_edge)
    along_y = axis_weights(offsets[1], corners[1], block_edge)
    along_z = axis_weights(offsets[2], corners[2], grid_depth)
    corner_weights = (
        along_x[:, None, None] * along_y[None, :, None] * along_z[None, None, :] * live_mask
    )
    return corner_weights.reshape(
        block_edge * block_edge, grid_depth, offsets.shape[1], slot_width
    ).astype(jnp.bfloat16)


def splat(weights, hidden):
    sums = jnp.einsum("czsp,hsp->sczh", weights, hidden, preferred_element_type=jnp.float32)
    return sums.astype(jnp.bfloat16).reshape(sums.shape[0], sums.shape[1], -1)


def interpolate(weights, blocks):
    cells = blocks.reshape(blocks.shape[0], weights.shape[0], weights.shape[1], -1)
    return jnp.einsum("czsp,sczh->hsp", weights, cells, preferred_element_type=jnp.float32).astype(
        jnp.bfloat16
    )


def band_kernel(w_ref, out_ref):
    width = w_ref.shape[2]
    depth = out_ref.shape[1] // width
    out_ref[...] = jnp.zeros_like(out_ref)
    for b in range(depth):
        low, high = max(b - 1, 0), min(b + 2, depth)
        out_ref[0, low * width : high * width, b * width : (b + 1) * width] = w_ref[
            0, (low - b + 1) * width : (high - b + 1) * width, :
        ]


def banded_weights(w_conv, grid_depth):
    layers, channels, outs = w_conv.shape[0], w_conv.shape[4], w_conv.shape[5]
    stacked = w_conv.reshape(layers * 9, 3 * channels, outs)
    return pl.pallas_call(
        band_kernel,
        grid=(layers * 9,),
        in_specs=[pl.BlockSpec((1, 3 * channels, outs), lambda n: (n, 0, 0))],
        out_specs=pl.BlockSpec((1, grid_depth * channels, grid_depth * outs), lambda n: (n, 0, 0)),
        out_shape=jax.ShapeDtypeStruct(
            (layers * 9, grid_depth * channels, grid_depth * outs), jnp.bfloat16
        ),
        cost_estimate=pl.CostEstimate(flops=0, bytes_accessed=20_000_000, transcendentals=0),
    )(stacked)


def halo_selectors():
    edge, nbx, nby = BLOCK_EDGE_CELLS, TX // BLOCK_EDGE_CELLS, TY // BLOCK_EDGE_CELLS
    blocks = nbx * nby
    lane = edge * max(nbx, nby)
    cut_sides = np.zeros((4, lane, edge * blocks), np.float32)
    cut_corners = np.zeros((4, lane, blocks), np.float32)
    for k, (da, db) in enumerate(DIRECTIONS):
        bx, by = (nbx - 1 if da > 0 else 0), (nby - 1 if db > 0 else 0)
        if db == 0:
            for j in range(edge):
                for y in range(nby):
                    cut_sides[k, j * nby + y, j * blocks + bx * nby + y] = 1
        elif da == 0:
            for i in range(edge):
                for x in range(nbx):
                    cut_sides[k, i * nbx + x, i * blocks + x * nby + by] = 1
        else:
            cut_corners[k - 4, :, bx * nby + by] = 1
    put_sides = np.zeros((4, edge, blocks, blocks + lane), np.float32)
    put_corners = np.zeros((4, blocks, blocks + 3 * lane), np.float32)
    for k, (da, db) in enumerate(DIRECTIONS):
        for x in range(nbx):
            for y in range(nby):
                row, sx, sy = x * nby + y, x - da, y - db
                out_x, out_y = not 0 <= sx < nbx, not 0 <= sy < nby
                if da == 0 or db == 0:
                    for phase in range(edge):
                        if out_x:
                            column = blocks + phase * nby + sy
                        elif out_y:
                            column = blocks + phase * nbx + sx
                        else:
                            column = sx * nby + sy
                        put_sides[k, phase, row, column] = 1
                else:
                    i, j = (edge - 1 if da > 0 else 0), (edge - 1 if db > 0 else 0)
                    if out_x and out_y:
                        column = blocks + 2 * lane
                    elif out_x:
                        column = blocks + j * nby + sy
                    elif out_y:
                        column = blocks + lane + i * nbx + sx
                    else:
                        column = sx * nby + sy
                    put_corners[k - 4, row, column] = 1
    return [jnp.asarray(m, jnp.bfloat16) for m in (cut_sides, cut_corners, put_sides, put_corners)]


def select(one_hot, values):
    return jnp.dot(one_hot, values, preferred_element_type=jnp.float32).astype(jnp.bfloat16)


def conv_kernel(
    sizes,
    arrived_ref,
    band_ref,
    cut_sides,
    cut_corners,
    put_sides,
    put_corners,
    out_ref,
    phases,
    around,
    leaving,
    landing,
    send_sem,
    recv_sem,
):
    rows, columns = sizes
    edge, blocks, every = BLOCK_EDGE_CELLS, phases.shape[2], phases.shape[3]
    layers = landing.shape[0]
    me_row, me_column = lax.axis_index("grid"), lax.axis_index("pts")

    def present(da, db):
        row, column = me_row + da, me_column + db
        return (row >= 0) & (row < rows) & (column >= 0) & (column < columns)

    barrier = pltpu.get_barrier_semaphore()
    for da, db in DIRECTIONS:

        @pl.when(present(da, db))
        def _():
            pl.semaphore_signal(
                barrier, inc=1, device_id=(me_column + db, me_row + da), device_id_type=MESH
            )

    queue = arrived_ref.shape[0]
    ids = arrived_ref[:, edge * edge * every :].astype(jnp.float32)[:, :blocks]
    places = lax.broadcasted_iota(jnp.int32, (queue, blocks), 1).astype(jnp.float32)
    picks = jnp.where(ids == places, 1.0, 0.0).astype(jnp.bfloat16)
    for cell in range(edge * edge):
        phases[cell // edge, cell % edge] = lax.dot_general(
            picks,
            arrived_ref[:, cell * every : (cell + 1) * every],
            (((0,), (0,)), ((), ())),
            preferred_element_type=jnp.float32,
        ).astype(jnp.bfloat16)

    tall = 3 - (me_row == 0).astype(jnp.int32) - (me_row == rows - 1).astype(jnp.int32)
    wide = 3 - (me_column == 0).astype(jnp.int32) - (me_column == columns - 1).astype(jnp.int32)
    pl.semaphore_wait(barrier, tall * wide - 1)

    for layer in range(layers):

        def copy(k):
            da, db = DIRECTIONS[k]
            return pltpu.make_async_remote_copy(
                src_ref=leaving.at[layer, k],
                dst_ref=landing.at[layer, k],
                send_sem=send_sem.at[layer, k],
                recv_sem=recv_sem.at[layer, k],
                device_id=(me_column + db, me_row + da),
                device_id_type=MESH,
            )

        for k, (da, db) in enumerate(DIRECTIONS):
            i, j = (edge - 1 if da > 0 else 0), (edge - 1 if db > 0 else 0)
            if db == 0:
                source = phases[i].reshape(edge * blocks, every)
            elif da == 0:
                source = phases[:, j].reshape(edge * blocks, every)
            else:
                source = phases[i, j]
            leaving[layer, k] = select(cut_sides[k] if k < 4 else cut_corners[k - 4], source)

            @pl.when(present(da, db))
            def _():
                copy(k).start()

        around[1 : edge + 1, 1 : edge + 1] = phases[...]
        for k, (da, db) in enumerate(DIRECTIONS):

            @pl.when(present(-da, -db))
            def _():
                copy(k).wait_recv()

            @pl.when(jnp.logical_not(present(-da, -db)))
            def _():
                landing[layer, k] = jnp.zeros(landing.shape[2:], landing.dtype)

        for k, (da, db) in enumerate(DIRECTIONS):
            to_x = 0 if da > 0 else edge + 1
            to_y = 0 if db > 0 else edge + 1
            i, j = (edge - 1 if da > 0 else 0), (edge - 1 if db > 0 else 0)
            if db == 0:
                for phase in range(edge):
                    around[to_x, phase + 1] = select(
                        put_sides[k, phase],
                        jnp.concatenate([phases[i, phase], landing[layer, k]], axis=0),
                    )
            elif da == 0:
                for phase in range(edge):
                    around[phase + 1, to_y] = select(
                        put_sides[k, phase],
                        jnp.concatenate([phases[phase, j], landing[layer, k]], axis=0),
                    )
            else:
                side_x = DIRECTIONS.index((da, 0))
                side_y = DIRECTIONS.index((0, db))
                around[to_x, to_y] = select(
                    put_corners[k - 4],
                    jnp.concatenate(
                        [
                            phases[i, j],
                            landing[layer, side_x],
                            landing[layer, side_y],
                            landing[layer, k],
                        ],
                        axis=0,
                    ),
                )

        def one_row(i, carry):
            total = jnp.zeros((edge * blocks, every), jnp.float32)
            for shift_x in range(3):
                for shift_y in range(3):
                    window = around[i + shift_x, shift_y : shift_y + edge]
                    total = total + jnp.dot(
                        window.reshape(edge * blocks, every),
                        band_ref[layer * 9 + shift_x * 3 + shift_y],
                        preferred_element_type=jnp.float32,
                    )
            activated = total / (1.0 + jnp.exp(-total))
            phases[i] = activated.astype(jnp.bfloat16).reshape(edge, blocks, every)
            return carry

        lax.fori_loop(0, edge, one_row, 0)

    for cell in range(edge * edge):
        out_ref[:, cell * every : (cell + 1) * every] = select(
            picks, phases[cell // edge, cell % edge]
        )
    for layer in range(layers):
        for k, (da, db) in enumerate(DIRECTIONS):

            @pl.when(present(da, db))
            def _():
                pltpu.make_async_remote_copy(
                    src_ref=leaving.at[layer, k],
                    dst_ref=landing.at[layer, k],
                    send_sem=send_sem.at[layer, k],
                    recv_sem=recv_sem.at[layer, k],
                    device_id=(me_column + db, me_row + da),
                    device_id_type=MESH,
                ).wait_send()


def convolve_blocks(arrived, banded, layers):
    edge = BLOCK_EDGE_CELLS
    blocks = (TX // edge) * (TY // edge)
    every = banded.shape[2]
    selectors = halo_selectors()
    halo = (layers, len(DIRECTIONS), selectors[0].shape[1], every)
    return pl.pallas_call(
        functools.partial(conv_kernel, (lax.axis_size("grid"), lax.axis_size("pts"))),
        out_shape=jax.ShapeDtypeStruct((arrived.shape[0], edge * edge * every), jnp.bfloat16),
        in_specs=[pl.BlockSpec(memory_space=pltpu.VMEM)] * 6,
        out_specs=pl.BlockSpec(memory_space=pltpu.VMEM),
        scratch_shapes=[
            pltpu.VMEM((edge, edge, blocks, every), jnp.bfloat16),
            pltpu.VMEM((edge + 2, edge + 2, blocks, every), jnp.bfloat16),
            pltpu.VMEM(halo, jnp.bfloat16),
            pltpu.VMEM(halo, jnp.bfloat16),
            pltpu.SemaphoreType.DMA(halo[:2]),
            pltpu.SemaphoreType.DMA(halo[:2]),
        ],
        compiler_params=pltpu.CompilerParams(collective_id=0, has_side_effects=True),
        cost_estimate=pl.CostEstimate(
            flops=layers * 18 * TX * TY * every * every,
            bytes_accessed=layers * 9 * every * every * 2,
            transcendentals=layers * TX * TY * every,
        ),
    )(arrived, banded, *selectors)


def per_device(
    features, w_in, w_mid, w_conv, point_frac, point_base, slot_dest, slot_tile_block, slot_count
):
    slot_total = slot_dest.shape[0]
    slot_width = features.shape[1] // slot_total
    owners = lax.axis_size("grid")
    per_owner = max(2, 2 * slot_total // owners)
    queue_length = owners * per_owner
    hidden_one = point_layer(w_in, features)
    hidden_two = point_layer(w_mid, hidden_one)
    channels = hidden_two.shape[0]
    hidden_two = hidden_two.reshape(channels, slot_total, slot_width)
    offsets = point_frac.reshape(3, slot_total, slot_width)
    corners = point_base.reshape(3, slot_total, slot_width)
    slot_order = jnp.arange(slot_total, dtype=jnp.int32)
    same_owner = (slot_dest[:, None] == slot_dest[None, :]) & (
        slot_order[None, :] < slot_order[:, None]
    )
    rank_within = jnp.sum(same_owner.astype(jnp.int32), axis=1)
    send_place = slot_dest * per_owner + rank_within
    send_match = send_place[None, :] == jnp.arange(queue_length, dtype=jnp.int32)[:, None]
    sent_block = jnp.sum(jnp.where(send_match, slot_tile_block[None, :] + 1, 0), axis=1) - 1
    send_picks = send_match.astype(jnp.bfloat16)
    banded = banded_weights(w_conv, GZ)
    weights = trilinear(offsets, corners, slot_count, BLOCK_EDGE_CELLS, GZ)
    local_sums = splat(weights, hidden_two).reshape(slot_total, -1)
    outgoing = jnp.dot(send_picks, local_sums, preferred_element_type=jnp.float32)
    outgoing = jnp.concatenate(
        [
            outgoing.astype(jnp.bfloat16),
            jnp.broadcast_to(sent_block[:, None], (queue_length, ID_LANES)).astype(jnp.bfloat16),
        ],
        axis=1,
    )
    arrived = lax.all_to_all(outgoing, "grid", split_axis=0, concat_axis=0, tiled=True)
    values = convolve_blocks(arrived, banded, w_conv.shape[0])
    returned = lax.all_to_all(values, "grid", split_axis=0, concat_axis=0, tiled=True)
    blocks = lax.dot_general(
        send_picks, returned, (((0,), (0,)), ((), ())), preferred_element_type=jnp.float32
    ).astype(jnp.bfloat16)
    interp = interpolate(weights, blocks)
    point_out = (hidden_two.astype(jnp.float32) + interp.astype(jnp.float32)).astype(jnp.bfloat16)
    return point_out.reshape(channels, slot_total * slot_width)


def solution(mesh):
    return jax.shard_map(
        per_device,
        mesh=mesh,
        in_specs=(
            P(None, ("pts", "grid")),
            P(),
            P(),
            P(),
            P(None, ("pts", "grid")),
            P(None, ("pts", "grid")),
            P(("pts", "grid")),
            P(("pts", "grid")),
            P(("pts", "grid")),
        ),
        out_specs=P(None, ("pts", "grid")),
        check_vma=False,
    )
```

```python
import functools

import jax
import jax.numpy as jnp
import numpy as np
from jax import lax
from jax.experimental import pallas as pl
from jax.experimental.pallas import tpu as pltpu
from jax.sharding import PartitionSpec as P

GZ = 8
BLOCK_EDGE_CELLS = 4
TX = 32
TY = 32
ID_LANES = 128
MESH = pl.DeviceIdType.MESH
DIRECTIONS = ((1, 0), (-1, 0), (0, 1), (0, -1), (1, 1), (1, -1), (-1, 1), (-1, -1))


def point_layer(weight, inputs):
    mixed_sum = lax.dot_general(
        weight, inputs, (((0,), (0,)), ((), ())), preferred_element_type=jnp.float32
    )
    return jax.nn.silu(mixed_sum).astype(jnp.bfloat16)


def axis_weights(offset, corner, length):
    positions = jnp.arange(length, dtype=jnp.int32)[:, None, None]
    below_part = jnp.where(positions == corner[None], 1.0 - offset[None], 0.0)
    above_part = jnp.where(positions == corner[None] + 1, offset[None], 0.0)
    return below_part + above_part


def trilinear(offsets, corners, counts, block_edge, grid_depth):
    slot_width = offsets.shape[2]
    live_mask = (jnp.arange(slot_width, dtype=jnp.int32)[None, :] < counts[:, None]).astype(
        jnp.float32
    )
    along_x = axis_weights(offsets[0], corners[0], block_edge)
    along_y = axis_weights(offsets[1], corners[1], block_edge)
    along_z = axis_weights(offsets[2], corners[2], grid_depth)
    corner_weights = (
        along_x[:, None, None] * along_y[None, :, None] * along_z[None, None, :] * live_mask
    )
    return corner_weights.reshape(
        block_edge * block_edge, grid_depth, offsets.shape[1], slot_width
    ).astype(jnp.bfloat16)


def splat(weights, hidden):
    sums = jnp.einsum("czsp,hsp->sczh", weights, hidden, preferred_element_type=jnp.float32)
    return sums.astype(jnp.bfloat16).reshape(sums.shape[0], sums.shape[1], -1)


def interpolate(weights, blocks):
    cells = blocks.reshape(blocks.shape[0], weights.shape[0], weights.shape[1], -1)
    return jnp.einsum("czsp,sczh->hsp", weights, cells, preferred_element_type=jnp.float32).astype(
        jnp.bfloat16
    )


def build_band(w_ref, band_ref):
    width = w_ref.shape[2]
    depth = band_ref.shape[1] // width

    def one(n, carry):
        band_ref[n] = jnp.zeros(band_ref.shape[1:], band_ref.dtype)
        for b in range(depth):
            low, high = max(b - 1, 0), min(b + 2, depth)
            band_ref[n, low * width : high * width, b * width : (b + 1) * width] = w_ref[
                n, (low - b + 1) * width : (high - b + 1) * width, :
            ]
        return carry

    lax.fori_loop(0, band_ref.shape[0], one, 0)


def halo_selectors():
    edge, nbx, nby = BLOCK_EDGE_CELLS, TX // BLOCK_EDGE_CELLS, TY // BLOCK_EDGE_CELLS
    blocks = nbx * nby
    lane = edge * max(nbx, nby)
    cut_sides = np.zeros((4, lane, edge * blocks), np.float32)
    cut_corners = np.zeros((4, lane, blocks), np.float32)
    for k, (da, db) in enumerate(DIRECTIONS):
        bx, by = (nbx - 1 if da > 0 else 0), (nby - 1 if db > 0 else 0)
        if db == 0:
            for j in range(edge):
                for y in range(nby):
                    cut_sides[k, j * nby + y, j * blocks + bx * nby + y] = 1
        elif da == 0:
            for i in range(edge):
                for x in range(nbx):
                    cut_sides[k, i * nbx + x, i * blocks + x * nby + by] = 1
        else:
            cut_corners[k - 4, :, bx * nby + by] = 1
    put_sides = np.zeros((4, edge, blocks, blocks + lane), np.float32)
    put_corners = np.zeros((4, blocks, blocks + 3 * lane), np.float32)
    for k, (da, db) in enumerate(DIRECTIONS):
        for x in range(nbx):
            for y in range(nby):
                row, sx, sy = x * nby + y, x - da, y - db
                out_x, out_y = not 0 <= sx < nbx, not 0 <= sy < nby
                if da == 0 or db == 0:
                    for phase in range(edge):
                        if out_x:
                            column = blocks + phase * nby + sy
                        elif out_y:
                            column = blocks + phase * nbx + sx
                        else:
                            column = sx * nby + sy
                        put_sides[k, phase, row, column] = 1
                else:
                    i, j = (edge - 1 if da > 0 else 0), (edge - 1 if db > 0 else 0)
                    if out_x and out_y:
                        column = blocks + 2 * lane
                    elif out_x:
                        column = blocks + j * nby + sy
                    elif out_y:
                        column = blocks + lane + i * nbx + sx
                    else:
                        column = sx * nby + sy
                    put_corners[k - 4, row, column] = 1
    return [jnp.asarray(m, jnp.bfloat16) for m in (cut_sides, cut_corners, put_sides, put_corners)]


def select(one_hot, values):
    return jnp.dot(one_hot, values, preferred_element_type=jnp.float32).astype(jnp.bfloat16)


def conv_kernel(
    sizes,
    outgoing_ref,
    w_ref,
    cut_sides,
    cut_corners,
    put_sides,
    put_corners,
    out_ref,
    arrived,
    values,
    band_ref,
    phases,
    around,
    leaving,
    landing,
    send_sem,
    recv_sem,
    go_send,
    go_recv,
    back_send,
    back_recv,
    own_sem,
):
    rows, columns = sizes
    edge, blocks, every = BLOCK_EDGE_CELLS, phases.shape[2], phases.shape[3]
    layers = landing.shape[0]
    me_row, me_column = lax.axis_index("grid"), lax.axis_index("pts")

    def present(da, db):
        row, column = me_row + da, me_column + db
        return (row >= 0) & (row < rows) & (column >= 0) & (column < columns)

    def go(t):
        owner = lax.rem(me_row + t, rows)
        return pltpu.make_async_remote_copy(
            src_ref=outgoing_ref.at[owner],
            dst_ref=arrived.at[me_row],
            send_sem=go_send.at[t],
            recv_sem=go_recv.at[t],
            device_id=(me_column, owner),
            device_id_type=MESH,
        )

    def back(i, t):
        origin = lax.rem(me_row + t, rows)
        part = pl.ds(i * edge * every, edge * every)
        return pltpu.make_async_remote_copy(
            src_ref=values.at[origin, :, part],
            dst_ref=out_ref.at[me_row, :, part],
            send_sem=back_send.at[i, t],
            recv_sem=back_recv.at[i, t],
            device_id=(me_column, origin),
            device_id_type=MESH,
        )

    def back_own(i):
        part = pl.ds(i * edge * every, edge * every)
        return pltpu.make_async_copy(
            values.at[me_row, :, part], out_ref.at[me_row, :, part], own_sem.at[i + 1]
        )

    barrier = pltpu.get_barrier_semaphore()
    for t in range(1, rows):
        pl.semaphore_signal(
            barrier,
            inc=1,
            device_id=(me_column, lax.rem(me_row + t, rows)),
            device_id_type=MESH,
        )
    for da, db in DIRECTIONS:
        if db != 0:

            @pl.when(present(da, db))
            def _():
                pl.semaphore_signal(
                    barrier, inc=1, device_id=(me_column + db, me_row + da), device_id_type=MESH
                )

    tall = 3 - (me_row == 0).astype(jnp.int32) - (me_row == rows - 1).astype(jnp.int32)
    wide = 2 - (me_column == 0).astype(jnp.int32) - (me_column == columns - 1).astype(jnp.int32)
    pl.semaphore_wait(barrier, rows - 1 + tall * wide)

    for t in range(1, rows):
        go(t).start()
    own = pltpu.make_async_copy(outgoing_ref.at[me_row], arrived.at[me_row], own_sem.at[0])
    own.start()
    build_band(w_ref, band_ref)
    own.wait()
    for t in range(1, rows):
        go(t).wait_recv()

    queue = arrived.shape[0] * arrived.shape[1]
    ids = arrived[:, :, edge * edge * every :].reshape(queue, ID_LANES)
    places = lax.broadcasted_iota(jnp.int32, (queue, blocks), 1).astype(jnp.float32)
    picks = jnp.where(ids.astype(jnp.float32)[:, :blocks] == places, 1.0, 0.0).astype(jnp.bfloat16)
    for cell in range(edge * edge):
        phases[cell // edge, cell % edge] = lax.dot_general(
            picks,
            arrived[:, :, cell * every : (cell + 1) * every].reshape(queue, every),
            (((0,), (0,)), ((), ())),
            preferred_element_type=jnp.float32,
        ).astype(jnp.bfloat16)

    for layer in range(layers):

        def copy(k):
            da, db = DIRECTIONS[k]
            return pltpu.make_async_remote_copy(
                src_ref=leaving.at[layer, k],
                dst_ref=landing.at[layer, k],
                send_sem=send_sem.at[layer, k],
                recv_sem=recv_sem.at[layer, k],
                device_id=(me_column + db, me_row + da),
                device_id_type=MESH,
            )

        for k, (da, db) in enumerate(DIRECTIONS):
            i, j = (edge - 1 if da > 0 else 0), (edge - 1 if db > 0 else 0)
            if db == 0:
                source = phases[i].reshape(edge * blocks, every)
            elif da == 0:
                source = phases[:, j].reshape(edge * blocks, every)
            else:
                source = phases[i, j]
            leaving[layer, k] = select(cut_sides[k] if k < 4 else cut_corners[k - 4], source)

            @pl.when(present(da, db))
            def _():
                copy(k).start()

        around[1 : edge + 1, 1 : edge + 1] = phases[...]
        for k, (da, db) in enumerate(DIRECTIONS):

            @pl.when(present(-da, -db))
            def _():
                copy(k).wait_recv()

            @pl.when(jnp.logical_not(present(-da, -db)))
            def _():
                landing[layer, k] = jnp.zeros(landing.shape[2:], landing.dtype)

        for k, (da, db) in enumerate(DIRECTIONS):
            to_x = 0 if da > 0 else edge + 1
            to_y = 0 if db > 0 else edge + 1
            i, j = (edge - 1 if da > 0 else 0), (edge - 1 if db > 0 else 0)
            if db == 0:
                for phase in range(edge):
                    around[to_x, phase + 1] = select(
                        put_sides[k, phase],
                        jnp.concatenate([phases[i, phase], landing[layer, k]], axis=0),
                    )
            elif da == 0:
                for phase in range(edge):
                    around[phase + 1, to_y] = select(
                        put_sides[k, phase],
                        jnp.concatenate([phases[phase, j], landing[layer, k]], axis=0),
                    )
            else:
                side_x = DIRECTIONS.index((da, 0))
                side_y = DIRECTIONS.index((0, db))
                around[to_x, to_y] = select(
                    put_corners[k - 4],
                    jnp.concatenate(
                        [
                            phases[i, j],
                            landing[layer, side_x],
                            landing[layer, side_y],
                            landing[layer, k],
                        ],
                        axis=0,
                    ),
                )

        def one_row(i, carry):
            total = jnp.zeros((edge * blocks, every), jnp.float32)
            for shift_x in range(3):
                for shift_y in range(3):
                    window = around[i + shift_x, shift_y : shift_y + edge]
                    total = total + jnp.dot(
                        window.reshape(edge * blocks, every),
                        band_ref[layer * 9 + shift_x * 3 + shift_y],
                        preferred_element_type=jnp.float32,
                    )
            activated = (total / (1.0 + jnp.exp(-total))).astype(jnp.bfloat16)
            phases[i] = activated.reshape(edge, blocks, every)
            return carry

        if layer < layers - 1:
            lax.fori_loop(0, edge, one_row, 0)
        else:
            for i in range(edge):
                one_row(i, 0)
                for j in range(edge):
                    cell = i * edge + j
                    values[:, :, cell * every : (cell + 1) * every] = select(
                        picks, phases[i, j]
                    ).reshape(values.shape[0], values.shape[1], every)
                for t in range(1, rows):
                    back(i, t).start()
                back_own(i).start()

    for t in range(1, rows):
        go(t).wait_send()
    for i in range(edge):
        back_own(i).wait()
        for t in range(1, rows):
            back(i, t).wait_recv()
            back(i, t).wait_send()
    for layer in range(layers):
        for k, (da, db) in enumerate(DIRECTIONS):

            @pl.when(present(da, db))
            def _():
                pltpu.make_async_remote_copy(
                    src_ref=leaving.at[layer, k],
                    dst_ref=landing.at[layer, k],
                    send_sem=send_sem.at[layer, k],
                    recv_sem=recv_sem.at[layer, k],
                    device_id=(me_column + db, me_row + da),
                    device_id_type=MESH,
                ).wait_send()


def exchange_and_convolve(outgoing, w_conv):
    edge = BLOCK_EDGE_CELLS
    blocks = (TX // edge) * (TY // edge)
    layers, channels, outs = w_conv.shape[0], w_conv.shape[4], w_conv.shape[5]
    every = GZ * channels
    rows, per_owner = outgoing.shape[:2]
    stacked = w_conv.reshape(layers * 9, 3 * channels, outs)
    selectors = halo_selectors()
    halo = (layers, len(DIRECTIONS), selectors[0].shape[1], every)
    queue = (rows, per_owner, edge * edge * every)
    return pl.pallas_call(
        functools.partial(conv_kernel, (lax.axis_size("grid"), lax.axis_size("pts"))),
        out_shape=jax.ShapeDtypeStruct(queue, jnp.bfloat16),
        in_specs=[pl.BlockSpec(memory_space=pltpu.VMEM)] * 6,
        out_specs=pl.BlockSpec(memory_space=pltpu.VMEM),
        scratch_shapes=[
            pltpu.VMEM(outgoing.shape, jnp.bfloat16),
            pltpu.VMEM(queue, jnp.bfloat16),
            pltpu.VMEM((layers * 9, every, every), jnp.bfloat16),
            pltpu.VMEM((edge, edge, blocks, every), jnp.bfloat16),
            pltpu.VMEM((edge + 2, edge + 2, blocks, every), jnp.bfloat16),
            pltpu.VMEM(halo, jnp.bfloat16),
            pltpu.VMEM(halo, jnp.bfloat16),
            pltpu.SemaphoreType.DMA(halo[:2]),
            pltpu.SemaphoreType.DMA(halo[:2]),
            pltpu.SemaphoreType.DMA((rows,)),
            pltpu.SemaphoreType.DMA((rows,)),
            pltpu.SemaphoreType.DMA((edge, rows)),
            pltpu.SemaphoreType.DMA((edge, rows)),
            pltpu.SemaphoreType.DMA((edge + 1,)),
        ],
        compiler_params=pltpu.CompilerParams(collective_id=0, has_side_effects=True),
    )(outgoing, stacked, *selectors)


def per_device(
    features, w_in, w_mid, w_conv, point_frac, point_base, slot_dest, slot_tile_block, slot_count
):
    slot_total = slot_dest.shape[0]
    slot_width = features.shape[1] // slot_total
    owners = lax.axis_size("grid")
    per_owner = max(2, 2 * slot_total // owners)
    queue_length = owners * per_owner
    hidden_one = point_layer(w_in, features)
    hidden_two = point_layer(w_mid, hidden_one)
    channels = hidden_two.shape[0]
    hidden_two = hidden_two.reshape(channels, slot_total, slot_width)
    offsets = point_frac.reshape(3, slot_total, slot_width)
    corners = point_base.reshape(3, slot_total, slot_width)
    slot_order = jnp.arange(slot_total, dtype=jnp.int32)
    same_owner = (slot_dest[:, None] == slot_dest[None, :]) & (
        slot_order[None, :] < slot_order[:, None]
    )
    rank_within = jnp.sum(same_owner.astype(jnp.int32), axis=1)
    send_place = slot_dest * per_owner + rank_within
    send_match = send_place[None, :] == jnp.arange(queue_length, dtype=jnp.int32)[:, None]
    sent_block = jnp.sum(jnp.where(send_match, slot_tile_block[None, :] + 1, 0), axis=1) - 1
    send_picks = send_match.astype(jnp.bfloat16)
    weights = trilinear(offsets, corners, slot_count, BLOCK_EDGE_CELLS, GZ)
    local_sums = splat(weights, hidden_two).reshape(slot_total, -1)
    outgoing = jnp.dot(send_picks, local_sums, preferred_element_type=jnp.float32)
    outgoing = jnp.concatenate(
        [
            outgoing.astype(jnp.bfloat16),
            jnp.broadcast_to(sent_block[:, None], (queue_length, ID_LANES)).astype(jnp.bfloat16),
        ],
        axis=1,
    )
    returned = exchange_and_convolve(outgoing.reshape(owners, per_owner, -1), w_conv)
    returned = returned.reshape(queue_length, -1)
    blocks = lax.dot_general(
        send_picks, returned, (((0,), (0,)), ((), ())), preferred_element_type=jnp.float32
    ).astype(jnp.bfloat16)
    interp = interpolate(weights, blocks)
    point_out = (hidden_two.astype(jnp.float32) + interp.astype(jnp.float32)).astype(jnp.bfloat16)
    return point_out.reshape(channels, slot_total * slot_width)


def solution(mesh):
    return jax.shard_map(
        per_device,
        mesh=mesh,
        in_specs=(
            P(None, ("pts", "grid")),
            P(),
            P(),
            P(),
            P(None, ("pts", "grid")),
            P(None, ("pts", "grid")),
            P(("pts", "grid")),
            P(("pts", "grid")),
            P(("pts", "grid")),
        ),
        out_specs=P(None, ("pts", "grid")),
        check_vma=False,
    )
```

```python
import functools

import jax
import jax.numpy as jnp
import numpy as np
from jax import lax
from jax.experimental import pallas as pl
from jax.experimental.pallas import tpu as pltpu
from jax.sharding import PartitionSpec as P

GZ = 8
BLOCK_EDGE_CELLS = 4
TX = 32
TY = 32
ID_LANES = 128
MESH = pl.DeviceIdType.MESH
DIRECTIONS = ((1, 0), (-1, 0), (0, 1), (0, -1), (1, 1), (1, -1), (-1, 1), (-1, -1))


def point_layer(weight, inputs):
    mixed_sum = lax.dot_general(
        weight, inputs, (((0,), (0,)), ((), ())), preferred_element_type=jnp.float32
    )
    return jax.nn.silu(mixed_sum).astype(jnp.bfloat16)


def axis_weights(offset, corner, length):
    positions = jnp.arange(length, dtype=jnp.int32)[:, None, None]
    below_part = jnp.where(positions == corner[None], 1.0 - offset[None], 0.0)
    above_part = jnp.where(positions == corner[None] + 1, offset[None], 0.0)
    return below_part + above_part


def trilinear(offsets, corners, counts, block_edge, grid_depth):
    slot_width = offsets.shape[2]
    live_mask = (jnp.arange(slot_width, dtype=jnp.int32)[None, :] < counts[:, None]).astype(
        jnp.float32
    )
    along_x = axis_weights(offsets[0], corners[0], block_edge)
    along_y = axis_weights(offsets[1], corners[1], block_edge)
    along_z = axis_weights(offsets[2], corners[2], grid_depth)
    corner_weights = (
        along_x[:, None, None] * along_y[None, :, None] * along_z[None, None, :] * live_mask
    )
    return corner_weights.reshape(
        block_edge * block_edge, grid_depth, offsets.shape[1], slot_width
    ).astype(jnp.bfloat16)


def splat(weights, hidden):
    sums = jnp.einsum("czsp,hsp->sczh", weights, hidden, preferred_element_type=jnp.float32)
    return sums.astype(jnp.bfloat16).reshape(sums.shape[0], sums.shape[1], -1)


def interpolate(weights, blocks):
    cells = blocks.reshape(blocks.shape[0], weights.shape[0], weights.shape[1], -1)
    return jnp.einsum("czsp,sczh->hsp", weights, cells, preferred_element_type=jnp.float32).astype(
        jnp.bfloat16
    )


def build_band(w_ref, band_ref):
    width = w_ref.shape[2]
    depth = band_ref.shape[1] // width

    def one(n, carry):
        band_ref[n] = jnp.zeros(band_ref.shape[1:], band_ref.dtype)
        for b in range(depth):
            low, high = max(b - 1, 0), min(b + 2, depth)
            band_ref[n, low * width : high * width, b * width : (b + 1) * width] = w_ref[
                n, (low - b + 1) * width : (high - b + 1) * width, :
            ]
        return carry

    lax.fori_loop(0, band_ref.shape[0], one, 0)


def halo_selectors():
    edge, nbx, nby = BLOCK_EDGE_CELLS, TX // BLOCK_EDGE_CELLS, TY // BLOCK_EDGE_CELLS
    blocks = nbx * nby
    lane = edge * max(nbx, nby)
    cut_sides = np.zeros((4, lane, edge * blocks), np.float32)
    cut_corners = np.zeros((4, lane, blocks), np.float32)
    for k, (da, db) in enumerate(DIRECTIONS):
        bx, by = (nbx - 1 if da > 0 else 0), (nby - 1 if db > 0 else 0)
        if db == 0:
            for j in range(edge):
                for y in range(nby):
                    cut_sides[k, j * nby + y, j * blocks + bx * nby + y] = 1
        elif da == 0:
            for i in range(edge):
                for x in range(nbx):
                    cut_sides[k, i * nbx + x, i * blocks + x * nby + by] = 1
        else:
            cut_corners[k - 4, :, bx * nby + by] = 1
    put_sides = np.zeros((4, edge, blocks, blocks + lane), np.float32)
    put_corners = np.zeros((4, blocks, blocks + 3 * lane), np.float32)
    for k, (da, db) in enumerate(DIRECTIONS):
        for x in range(nbx):
            for y in range(nby):
                row, sx, sy = x * nby + y, x - da, y - db
                out_x, out_y = not 0 <= sx < nbx, not 0 <= sy < nby
                if da == 0 or db == 0:
                    for phase in range(edge):
                        if out_x:
                            column = blocks + phase * nby + sy
                        elif out_y:
                            column = blocks + phase * nbx + sx
                        else:
                            column = sx * nby + sy
                        put_sides[k, phase, row, column] = 1
                else:
                    i, j = (edge - 1 if da > 0 else 0), (edge - 1 if db > 0 else 0)
                    if out_x and out_y:
                        column = blocks + 2 * lane
                    elif out_x:
                        column = blocks + j * nby + sy
                    elif out_y:
                        column = blocks + lane + i * nbx + sx
                    else:
                        column = sx * nby + sy
                    put_corners[k - 4, row, column] = 1
    return [jnp.asarray(m, jnp.bfloat16) for m in (cut_sides, cut_corners, put_sides, put_corners)]


def select(one_hot, values):
    return jnp.dot(one_hot, values, preferred_element_type=jnp.float32).astype(jnp.bfloat16)


def conv_kernel(
    sizes,
    ids_ref,
    outgoing_ref,
    w_ref,
    cut_sides,
    cut_corners,
    put_sides,
    put_corners,
    out_ref,
    ids,
    arrived,
    values,
    totals,
    band_ref,
    phases,
    around,
    leaving,
    landing,
    send_sem,
    recv_sem,
    id_send,
    id_recv,
    go_send,
    go_recv,
    back_send,
    back_recv,
    own_sem,
):
    rows, columns = sizes
    edge, blocks, every = BLOCK_EDGE_CELLS, phases.shape[2], phases.shape[3]
    layers = landing.shape[0]
    me_row, me_column = lax.axis_index("grid"), lax.axis_index("pts")

    def present(da, db):
        row, column = me_row + da, me_column + db
        return (row >= 0) & (row < rows) & (column >= 0) & (column < columns)

    def tell(t):
        owner = lax.rem(me_row + t, rows)
        return pltpu.make_async_remote_copy(
            src_ref=ids_ref.at[owner],
            dst_ref=ids.at[me_row],
            send_sem=id_send.at[t],
            recv_sem=id_recv.at[t],
            device_id=(me_column, owner),
            device_id_type=MESH,
        )

    def go(i, t):
        owner = lax.rem(me_row + t, rows)
        part = pl.ds(i * edge * every, edge * every)
        return pltpu.make_async_remote_copy(
            src_ref=outgoing_ref.at[owner, :, part],
            dst_ref=arrived.at[me_row, :, part],
            send_sem=go_send.at[i, t],
            recv_sem=go_recv.at[i, t],
            device_id=(me_column, owner),
            device_id_type=MESH,
        )

    def back(i, t):
        origin = lax.rem(me_row + t, rows)
        part = pl.ds(i * edge * every, edge * every)
        return pltpu.make_async_remote_copy(
            src_ref=values.at[origin, :, part],
            dst_ref=out_ref.at[me_row, :, part],
            send_sem=back_send.at[i, t],
            recv_sem=back_recv.at[i, t],
            device_id=(me_column, origin),
            device_id_type=MESH,
        )

    def back_own(i):
        part = pl.ds(i * edge * every, edge * every)
        return pltpu.make_async_copy(
            values.at[me_row, :, part], out_ref.at[me_row, :, part], own_sem.at[i + 1]
        )

    barrier = pltpu.get_barrier_semaphore()
    for t in range(1, rows):
        pl.semaphore_signal(
            barrier,
            inc=1,
            device_id=(me_column, lax.rem(me_row + t, rows)),
            device_id_type=MESH,
        )
    for da, db in DIRECTIONS:
        if db != 0:

            @pl.when(present(da, db))
            def _():
                pl.semaphore_signal(
                    barrier, inc=1, device_id=(me_column + db, me_row + da), device_id_type=MESH
                )

    tall = 3 - (me_row == 0).astype(jnp.int32) - (me_row == rows - 1).astype(jnp.int32)
    wide = 2 - (me_column == 0).astype(jnp.int32) - (me_column == columns - 1).astype(jnp.int32)
    pl.semaphore_wait(barrier, rows - 1 + tall * wide)

    for t in range(1, rows):
        tell(t).start()
    for i in range(edge):
        for t in range(1, rows):
            go(i, t).start()
    own = pltpu.make_async_copy(outgoing_ref.at[me_row], arrived.at[me_row], own_sem.at[0])
    own.start()
    ids[me_row] = ids_ref[me_row]
    build_band(w_ref, band_ref)

    def inner_terms(layer, source):
        window = around[source + 1, 1 : edge + 1].reshape(edge * blocks, every)
        for shift_x in range(3):
            i = source + 1 - shift_x
            if 0 <= i < edge:
                term = jnp.dot(
                    window,
                    band_ref[layer * 9 + shift_x * 3 + 1],
                    preferred_element_type=jnp.float32,
                )
                if source == max(i - 1, 0):
                    totals[i] = term
                else:
                    totals[i] += term

    own.wait()
    for t in range(1, rows):
        tell(t).wait_recv()
    queue = arrived.shape[0] * arrived.shape[1]
    named = ids[...].reshape(queue, ID_LANES).astype(jnp.float32)[:, :blocks]
    places = lax.broadcasted_iota(jnp.int32, (queue, blocks), 1).astype(jnp.float32)
    picks = jnp.where(named == places, 1.0, 0.0).astype(jnp.bfloat16)
    for i in range(edge):
        for t in range(1, rows):
            go(i, t).wait_recv()
        for j in range(edge):
            cell = i * edge + j
            phases[i, j] = lax.dot_general(
                picks,
                arrived[:, :, cell * every : (cell + 1) * every].reshape(queue, every),
                (((0,), (0,)), ((), ())),
                preferred_element_type=jnp.float32,
            ).astype(jnp.bfloat16)
        around[i + 1, 1 : edge + 1] = phases[i]
        if i < edge - 1:
            inner_terms(0, i)

    for layer in range(layers):

        def copy(k):
            da, db = DIRECTIONS[k]
            return pltpu.make_async_remote_copy(
                src_ref=leaving.at[layer, k],
                dst_ref=landing.at[layer, k],
                send_sem=send_sem.at[layer, k],
                recv_sem=recv_sem.at[layer, k],
                device_id=(me_column + db, me_row + da),
                device_id_type=MESH,
            )

        for k, (da, db) in enumerate(DIRECTIONS):
            i, j = (edge - 1 if da > 0 else 0), (edge - 1 if db > 0 else 0)
            if db == 0:
                source = phases[i].reshape(edge * blocks, every)
            elif da == 0:
                source = phases[:, j].reshape(edge * blocks, every)
            else:
                source = phases[i, j]
            leaving[layer, k] = select(cut_sides[k] if k < 4 else cut_corners[k - 4], source)

            @pl.when(present(da, db))
            def _():
                copy(k).start()

        if layer == 0:
            inner_terms(0, edge - 1)
        else:
            for i in range(edge):
                around[i + 1, 1 : edge + 1] = phases[i]
                inner_terms(layer, i)
        for k, (da, db) in enumerate(DIRECTIONS):

            @pl.when(present(-da, -db))
            def _():
                copy(k).wait_recv()

            @pl.when(jnp.logical_not(present(-da, -db)))
            def _():
                landing[layer, k] = jnp.zeros(landing.shape[2:], landing.dtype)

        for k, (da, db) in enumerate(DIRECTIONS):
            to_x = 0 if da > 0 else edge + 1
            to_y = 0 if db > 0 else edge + 1
            i, j = (edge - 1 if da > 0 else 0), (edge - 1 if db > 0 else 0)
            if db == 0:
                for phase in range(edge):
                    around[to_x, phase + 1] = select(
                        put_sides[k, phase],
                        jnp.concatenate([phases[i, phase], landing[layer, k]], axis=0),
                    )
            elif da == 0:
                for phase in range(edge):
                    around[phase + 1, to_y] = select(
                        put_sides[k, phase],
                        jnp.concatenate([phases[phase, j], landing[layer, k]], axis=0),
                    )
            else:
                side_x = DIRECTIONS.index((da, 0))
                side_y = DIRECTIONS.index((0, db))
                around[to_x, to_y] = select(
                    put_corners[k - 4],
                    jnp.concatenate(
                        [
                            phases[i, j],
                            landing[layer, side_x],
                            landing[layer, side_y],
                            landing[layer, k],
                        ],
                        axis=0,
                    ),
                )

        for i in range(edge):
            total = totals[i]
            for shift_x in range(3):
                for shift_y in range(3):
                    if shift_y == 1 and 1 <= i + shift_x <= edge:
                        continue
                    window = around[i + shift_x, shift_y : shift_y + edge]
                    total = total + jnp.dot(
                        window.reshape(edge * blocks, every),
                        band_ref[layer * 9 + shift_x * 3 + shift_y],
                        preferred_element_type=jnp.float32,
                    )
            activated = (total / (1.0 + jnp.exp(-total))).astype(jnp.bfloat16)
            phases[i] = activated.reshape(edge, blocks, every)
            if layer == layers - 1:
                for j in range(edge):
                    cell = i * edge + j
                    values[:, :, cell * every : (cell + 1) * every] = select(
                        picks, phases[i, j]
                    ).reshape(values.shape[0], values.shape[1], every)
                for t in range(1, rows):
                    back(i, t).start()
                back_own(i).start()

    for t in range(1, rows):
        tell(t).wait_send()
        for i in range(edge):
            go(i, t).wait_send()
    for i in range(edge):
        back_own(i).wait()
        for t in range(1, rows):
            back(i, t).wait_recv()
            back(i, t).wait_send()
    for layer in range(layers):
        for k, (da, db) in enumerate(DIRECTIONS):

            @pl.when(present(da, db))
            def _():
                pltpu.make_async_remote_copy(
                    src_ref=leaving.at[layer, k],
                    dst_ref=landing.at[layer, k],
                    send_sem=send_sem.at[layer, k],
                    recv_sem=recv_sem.at[layer, k],
                    device_id=(me_column + db, me_row + da),
                    device_id_type=MESH,
                ).wait_send()


def exchange_and_convolve(sent_ids, outgoing, w_conv):
    edge = BLOCK_EDGE_CELLS
    blocks = (TX // edge) * (TY // edge)
    layers, channels, outs = w_conv.shape[0], w_conv.shape[4], w_conv.shape[5]
    every = GZ * channels
    rows, per_owner = outgoing.shape[:2]
    stacked = w_conv.reshape(layers * 9, 3 * channels, outs)
    selectors = halo_selectors()
    halo = (layers, len(DIRECTIONS), selectors[0].shape[1], every)
    queue = (rows, per_owner, edge * edge * every)
    return pl.pallas_call(
        functools.partial(conv_kernel, (lax.axis_size("grid"), lax.axis_size("pts"))),
        out_shape=jax.ShapeDtypeStruct(queue, jnp.bfloat16),
        in_specs=[pl.BlockSpec(memory_space=pltpu.VMEM)] * 7,
        out_specs=pl.BlockSpec(memory_space=pltpu.VMEM),
        scratch_shapes=[
            pltpu.VMEM(sent_ids.shape, jnp.bfloat16),
            pltpu.VMEM(queue, jnp.bfloat16),
            pltpu.VMEM(queue, jnp.bfloat16),
            pltpu.VMEM((edge, edge * blocks, every), jnp.float32),
            pltpu.VMEM((layers * 9, every, every), jnp.bfloat16),
            pltpu.VMEM((edge, edge, blocks, every), jnp.bfloat16),
            pltpu.VMEM((edge + 2, edge + 2, blocks, every), jnp.bfloat16),
            pltpu.VMEM(halo, jnp.bfloat16),
            pltpu.VMEM(halo, jnp.bfloat16),
            pltpu.SemaphoreType.DMA(halo[:2]),
            pltpu.SemaphoreType.DMA(halo[:2]),
            pltpu.SemaphoreType.DMA((rows,)),
            pltpu.SemaphoreType.DMA((rows,)),
            pltpu.SemaphoreType.DMA((edge, rows)),
            pltpu.SemaphoreType.DMA((edge, rows)),
            pltpu.SemaphoreType.DMA((edge, rows)),
            pltpu.SemaphoreType.DMA((edge, rows)),
            pltpu.SemaphoreType.DMA((edge + 1,)),
        ],
        compiler_params=pltpu.CompilerParams(collective_id=0, has_side_effects=True),
    )(sent_ids, outgoing, stacked, *selectors)


def per_device(
    features, w_in, w_mid, w_conv, point_frac, point_base, slot_dest, slot_tile_block, slot_count
):
    slot_total = slot_dest.shape[0]
    slot_width = features.shape[1] // slot_total
    owners = lax.axis_size("grid")
    per_owner = max(2, 2 * slot_total // owners)
    queue_length = owners * per_owner
    hidden_one = point_layer(w_in, features)
    hidden_two = point_layer(w_mid, hidden_one)
    channels = hidden_two.shape[0]
    hidden_two = hidden_two.reshape(channels, slot_total, slot_width)
    offsets = point_frac.reshape(3, slot_total, slot_width)
    corners = point_base.reshape(3, slot_total, slot_width)
    slot_order = jnp.arange(slot_total, dtype=jnp.int32)
    same_owner = (slot_dest[:, None] == slot_dest[None, :]) & (
        slot_order[None, :] < slot_order[:, None]
    )
    rank_within = jnp.sum(same_owner.astype(jnp.int32), axis=1)
    send_place = slot_dest * per_owner + rank_within
    send_match = send_place[None, :] == jnp.arange(queue_length, dtype=jnp.int32)[:, None]
    sent_block = jnp.sum(jnp.where(send_match, slot_tile_block[None, :] + 1, 0), axis=1) - 1
    send_picks = send_match.astype(jnp.bfloat16)
    weights = trilinear(offsets, corners, slot_count, BLOCK_EDGE_CELLS, GZ)
    local_sums = splat(weights, hidden_two).reshape(slot_total, -1)
    outgoing = jnp.dot(send_picks, local_sums, preferred_element_type=jnp.float32)
    sent_ids = jnp.broadcast_to(sent_block[:, None], (queue_length, ID_LANES)).astype(jnp.bfloat16)
    returned = exchange_and_convolve(
        sent_ids.reshape(owners, per_owner, ID_LANES),
        outgoing.astype(jnp.bfloat16).reshape(owners, per_owner, -1),
        w_conv,
    )
    returned = returned.reshape(queue_length, -1)
    blocks = lax.dot_general(
        send_picks, returned, (((0,), (0,)), ((), ())), preferred_element_type=jnp.float32
    ).astype(jnp.bfloat16)
    interp = interpolate(weights, blocks)
    point_out = (hidden_two.astype(jnp.float32) + interp.astype(jnp.float32)).astype(jnp.bfloat16)
    return point_out.reshape(channels, slot_total * slot_width)


def solution(mesh):
    return jax.shard_map(
        per_device,
        mesh=mesh,
        in_specs=(
            P(None, ("pts", "grid")),
            P(),
            P(),
            P(),
            P(None, ("pts", "grid")),
            P(None, ("pts", "grid")),
            P(("pts", "grid")),
            P(("pts", "grid")),
            P(("pts", "grid")),
        ),
        out_specs=P(None, ("pts", "grid")),
        check_vma=False,
    )
```

```python
import functools

import jax
import jax.numpy as jnp
import numpy as np
from jax import lax
from jax.experimental import pallas as pl
from jax.experimental.pallas import tpu as pltpu
from jax.sharding import PartitionSpec as P

GZ = 8
BLOCK_EDGE_CELLS = 4
TX = 32
TY = 32
ID_LANES = 128
MESH = pl.DeviceIdType.MESH
DIRECTIONS = ((1, 0), (-1, 0), (0, 1), (0, -1), (1, 1), (1, -1), (-1, 1), (-1, -1))


def point_layer(weight, inputs):
    mixed_sum = lax.dot_general(
        weight, inputs, (((0,), (0,)), ((), ())), preferred_element_type=jnp.float32
    )
    return jax.nn.silu(mixed_sum).astype(jnp.bfloat16)


def axis_weights(offset, corner, length):
    positions = jnp.arange(length, dtype=jnp.int32)[:, None, None]
    below_part = jnp.where(positions == corner[None], 1.0 - offset[None], 0.0)
    above_part = jnp.where(positions == corner[None] + 1, offset[None], 0.0)
    return below_part + above_part


def trilinear(offsets, corners, counts, block_edge, grid_depth):
    slot_width = offsets.shape[2]
    live_mask = (jnp.arange(slot_width, dtype=jnp.int32)[None, :] < counts[:, None]).astype(
        jnp.float32
    )
    along_x = axis_weights(offsets[0], corners[0], block_edge)
    along_y = axis_weights(offsets[1], corners[1], block_edge)
    along_z = axis_weights(offsets[2], corners[2], grid_depth)
    corner_weights = (
        along_x[:, None, None] * along_y[None, :, None] * along_z[None, None, :] * live_mask
    )
    return corner_weights.reshape(
        block_edge * block_edge, grid_depth, offsets.shape[1], slot_width
    ).astype(jnp.bfloat16)


def splat(weights, hidden):
    sums = jnp.einsum("czsp,hsp->sczh", weights, hidden, preferred_element_type=jnp.float32)
    return sums.astype(jnp.bfloat16).reshape(sums.shape[0], sums.shape[1], -1)


def interpolate(weights, blocks):
    cells = blocks.reshape(blocks.shape[0], weights.shape[0], weights.shape[1], -1)
    return jnp.einsum("czsp,sczh->hsp", weights, cells, preferred_element_type=jnp.float32).astype(
        jnp.bfloat16
    )


def build_band(w_ref, band_ref):
    width = w_ref.shape[2]
    depth = band_ref.shape[1] // width

    def one(n, carry):
        band_ref[n] = jnp.zeros(band_ref.shape[1:], band_ref.dtype)
        for b in range(depth):
            low, high = max(b - 1, 0), min(b + 2, depth)
            band_ref[n, low * width : high * width, b * width : (b + 1) * width] = w_ref[
                n, (low - b + 1) * width : (high - b + 1) * width, :
            ]
        return carry

    lax.fori_loop(0, band_ref.shape[0], one, 0)


def halo_selectors():
    edge, nbx, nby = BLOCK_EDGE_CELLS, TX // BLOCK_EDGE_CELLS, TY // BLOCK_EDGE_CELLS
    blocks = nbx * nby
    lane = edge * max(nbx, nby)
    cut_sides = np.zeros((4, lane, edge * blocks), np.float32)
    cut_corners = np.zeros((4, lane, blocks), np.float32)
    for k, (da, db) in enumerate(DIRECTIONS):
        bx, by = (nbx - 1 if da > 0 else 0), (nby - 1 if db > 0 else 0)
        if db == 0:
            for j in range(edge):
                for y in range(nby):
                    cut_sides[k, j * nby + y, j * blocks + bx * nby + y] = 1
        elif da == 0:
            for i in range(edge):
                for x in range(nbx):
                    cut_sides[k, i * nbx + x, i * blocks + x * nby + by] = 1
        else:
            cut_corners[k - 4, :, bx * nby + by] = 1
    put_sides = np.zeros((4, edge, blocks, blocks + lane), np.float32)
    put_corners = np.zeros((4, blocks, blocks + 3 * lane), np.float32)
    for k, (da, db) in enumerate(DIRECTIONS):
        for x in range(nbx):
            for y in range(nby):
                row, sx, sy = x * nby + y, x - da, y - db
                out_x, out_y = not 0 <= sx < nbx, not 0 <= sy < nby
                if da == 0 or db == 0:
                    for phase in range(edge):
                        if out_x:
                            column = blocks + phase * nby + sy
                        elif out_y:
                            column = blocks + phase * nbx + sx
                        else:
                            column = sx * nby + sy
                        put_sides[k, phase, row, column] = 1
                else:
                    i, j = (edge - 1 if da > 0 else 0), (edge - 1 if db > 0 else 0)
                    if out_x and out_y:
                        column = blocks + 2 * lane
                    elif out_x:
                        column = blocks + j * nby + sy
                    elif out_y:
                        column = blocks + lane + i * nbx + sx
                    else:
                        column = sx * nby + sy
                    put_corners[k - 4, row, column] = 1
    return [jnp.asarray(m, jnp.bfloat16) for m in (cut_sides, cut_corners, put_sides, put_corners)]


def select(one_hot, values):
    return jnp.dot(one_hot, values, preferred_element_type=jnp.float32).astype(jnp.bfloat16)


def conv_kernel(
    sizes,
    ids_ref,
    send_picks,
    sums_ref,
    w_ref,
    cut_sides,
    cut_corners,
    put_sides,
    put_corners,
    out_ref,
    ids,
    outgoing,
    arrived,
    values,
    returned,
    totals,
    band_ref,
    phases,
    around,
    leaving,
    landing,
    send_sem,
    recv_sem,
    id_send,
    id_recv,
    go_send,
    go_recv,
    back_send,
    back_recv,
    own_sem,
):
    rows, columns = sizes
    edge, blocks, every = BLOCK_EDGE_CELLS, phases.shape[2], phases.shape[3]
    layers = landing.shape[0]
    me_row, me_column = lax.axis_index("grid"), lax.axis_index("pts")

    def present(da, db):
        row, column = me_row + da, me_column + db
        return (row >= 0) & (row < rows) & (column >= 0) & (column < columns)

    def tell(t):
        owner = lax.rem(me_row + t, rows)
        return pltpu.make_async_remote_copy(
            src_ref=ids_ref.at[owner],
            dst_ref=ids.at[me_row],
            send_sem=id_send.at[t],
            recv_sem=id_recv.at[t],
            device_id=(me_column, owner),
            device_id_type=MESH,
        )

    def go(i, t):
        owner = lax.rem(me_row + t, rows)
        part = pl.ds(i * edge * every, edge * every)
        return pltpu.make_async_remote_copy(
            src_ref=outgoing.at[owner, :, part],
            dst_ref=arrived.at[me_row, :, part],
            send_sem=go_send.at[i, t],
            recv_sem=go_recv.at[i, t],
            device_id=(me_column, owner),
            device_id_type=MESH,
        )

    def back(i, t):
        origin = lax.rem(me_row + t, rows)
        part = pl.ds(i * edge * every, edge * every)
        return pltpu.make_async_remote_copy(
            src_ref=values.at[origin, :, part],
            dst_ref=returned.at[me_row, :, part],
            send_sem=back_send.at[i, t],
            recv_sem=back_recv.at[i, t],
            device_id=(me_column, origin),
            device_id_type=MESH,
        )

    def back_own(i):
        part = pl.ds(i * edge * every, edge * every)
        return pltpu.make_async_copy(
            values.at[me_row, :, part], returned.at[me_row, :, part], own_sem.at[i + 1]
        )

    barrier = pltpu.get_barrier_semaphore()
    for t in range(1, rows):
        pl.semaphore_signal(
            barrier,
            inc=1,
            device_id=(me_column, lax.rem(me_row + t, rows)),
            device_id_type=MESH,
        )
    for da, db in DIRECTIONS:
        if db != 0:

            @pl.when(present(da, db))
            def _():
                pl.semaphore_signal(
                    barrier, inc=1, device_id=(me_column + db, me_row + da), device_id_type=MESH
                )

    tall = 3 - (me_row == 0).astype(jnp.int32) - (me_row == rows - 1).astype(jnp.int32)
    wide = 2 - (me_column == 0).astype(jnp.int32) - (me_column == columns - 1).astype(jnp.int32)
    pl.semaphore_wait(barrier, rows - 1 + tall * wide)

    for t in range(1, rows):
        tell(t).start()
    for i in range(edge):
        for j in range(edge):
            lanes = slice((i * edge + j) * every, (i * edge + j + 1) * every)
            outgoing[:, :, lanes] = select(send_picks[...], sums_ref[:, lanes]).reshape(
                outgoing.shape[0], outgoing.shape[1], every
            )
        for t in range(1, rows):
            go(i, t).start()
    own = pltpu.make_async_copy(outgoing.at[me_row], arrived.at[me_row], own_sem.at[0])
    own.start()
    ids[me_row] = ids_ref[me_row]
    build_band(w_ref, band_ref)

    def inner_terms(layer, source):
        window = around[source + 1, 1 : edge + 1].reshape(edge * blocks, every)
        for shift_x in range(3):
            i = source + 1 - shift_x
            if 0 <= i < edge:
                term = jnp.dot(
                    window,
                    band_ref[layer * 9 + shift_x * 3 + 1],
                    preferred_element_type=jnp.float32,
                )
                if source == max(i - 1, 0):
                    totals[i] = term
                else:
                    totals[i] += term

    own.wait()
    for t in range(1, rows):
        tell(t).wait_recv()
    queue = arrived.shape[0] * arrived.shape[1]
    named = ids[...].reshape(queue, ID_LANES).astype(jnp.float32)[:, :blocks]
    places = lax.broadcasted_iota(jnp.int32, (queue, blocks), 1).astype(jnp.float32)
    picks = jnp.where(named == places, 1.0, 0.0).astype(jnp.bfloat16)
    for i in range(edge):
        for t in range(1, rows):
            go(i, t).wait_recv()
        for j in range(edge):
            cell = i * edge + j
            phases[i, j] = lax.dot_general(
                picks,
                arrived[:, :, cell * every : (cell + 1) * every].reshape(queue, every),
                (((0,), (0,)), ((), ())),
                preferred_element_type=jnp.float32,
            ).astype(jnp.bfloat16)
        around[i + 1, 1 : edge + 1] = phases[i]
        if i < edge - 1:
            inner_terms(0, i)

    for layer in range(layers):

        def copy(k):
            da, db = DIRECTIONS[k]
            return pltpu.make_async_remote_copy(
                src_ref=leaving.at[layer, k],
                dst_ref=landing.at[layer, k],
                send_sem=send_sem.at[layer, k],
                recv_sem=recv_sem.at[layer, k],
                device_id=(me_column + db, me_row + da),
                device_id_type=MESH,
            )

        for k, (da, db) in enumerate(DIRECTIONS):
            i, j = (edge - 1 if da > 0 else 0), (edge - 1 if db > 0 else 0)
            if db == 0:
                source = phases[i].reshape(edge * blocks, every)
            elif da == 0:
                source = phases[:, j].reshape(edge * blocks, every)
            else:
                source = phases[i, j]
            leaving[layer, k] = select(cut_sides[k] if k < 4 else cut_corners[k - 4], source)

            @pl.when(present(da, db))
            def _():
                copy(k).start()

        if layer == 0:
            inner_terms(0, edge - 1)
        else:
            for i in range(edge):
                around[i + 1, 1 : edge + 1] = phases[i]
                inner_terms(layer, i)
        for k, (da, db) in enumerate(DIRECTIONS):

            @pl.when(present(-da, -db))
            def _():
                copy(k).wait_recv()

            @pl.when(jnp.logical_not(present(-da, -db)))
            def _():
                landing[layer, k] = jnp.zeros(landing.shape[2:], landing.dtype)

        for k, (da, db) in enumerate(DIRECTIONS):
            to_x = 0 if da > 0 else edge + 1
            to_y = 0 if db > 0 else edge + 1
            i, j = (edge - 1 if da > 0 else 0), (edge - 1 if db > 0 else 0)
            if db == 0:
                for phase in range(edge):
                    around[to_x, phase + 1] = select(
                        put_sides[k, phase],
                        jnp.concatenate([phases[i, phase], landing[layer, k]], axis=0),
                    )
            elif da == 0:
                for phase in range(edge):
                    around[phase + 1, to_y] = select(
                        put_sides[k, phase],
                        jnp.concatenate([phases[phase, j], landing[layer, k]], axis=0),
                    )
            else:
                side_x = DIRECTIONS.index((da, 0))
                side_y = DIRECTIONS.index((0, db))
                around[to_x, to_y] = select(
                    put_corners[k - 4],
                    jnp.concatenate(
                        [
                            phases[i, j],
                            landing[layer, side_x],
                            landing[layer, side_y],
                            landing[layer, k],
                        ],
                        axis=0,
                    ),
                )

        for i in range(edge):
            total = totals[i]
            for shift_x in range(3):
                for shift_y in range(3):
                    if shift_y == 1 and 1 <= i + shift_x <= edge:
                        continue
                    window = around[i + shift_x, shift_y : shift_y + edge]
                    total = total + jnp.dot(
                        window.reshape(edge * blocks, every),
                        band_ref[layer * 9 + shift_x * 3 + shift_y],
                        preferred_element_type=jnp.float32,
                    )
            activated = (total / (1.0 + jnp.exp(-total))).astype(jnp.bfloat16)
            phases[i] = activated.reshape(edge, blocks, every)
            if layer == layers - 1:
                for j in range(edge):
                    cell = i * edge + j
                    values[:, :, cell * every : (cell + 1) * every] = select(
                        picks, phases[i, j]
                    ).reshape(values.shape[0], values.shape[1], every)
                for t in range(1, rows):
                    back(i, t).start()
                back_own(i).start()

    for t in range(1, rows):
        tell(t).wait_send()
        for i in range(edge):
            go(i, t).wait_send()
    for i in range(edge):
        back_own(i).wait()
        for t in range(1, rows):
            back(i, t).wait_recv()
        for j in range(edge):
            lanes = slice((i * edge + j) * every, (i * edge + j + 1) * every)
            out_ref[:, lanes] = lax.dot_general(
                send_picks[...],
                returned[:, :, lanes].reshape(queue, every),
                (((0,), (0,)), ((), ())),
                preferred_element_type=jnp.float32,
            ).astype(jnp.bfloat16)
    for i in range(edge):
        for t in range(1, rows):
            back(i, t).wait_send()
    for layer in range(layers):
        for k, (da, db) in enumerate(DIRECTIONS):

            @pl.when(present(da, db))
            def _():
                pltpu.make_async_remote_copy(
                    src_ref=leaving.at[layer, k],
                    dst_ref=landing.at[layer, k],
                    send_sem=send_sem.at[layer, k],
                    recv_sem=recv_sem.at[layer, k],
                    device_id=(me_column + db, me_row + da),
                    device_id_type=MESH,
                ).wait_send()


def exchange_and_convolve(sent_ids, send_picks, local_sums, w_conv):
    edge = BLOCK_EDGE_CELLS
    blocks = (TX // edge) * (TY // edge)
    layers, channels, outs = w_conv.shape[0], w_conv.shape[4], w_conv.shape[5]
    every = GZ * channels
    rows, per_owner = sent_ids.shape[:2]
    stacked = w_conv.reshape(layers * 9, 3 * channels, outs)
    selectors = halo_selectors()
    halo = (layers, len(DIRECTIONS), selectors[0].shape[1], every)
    queue = (rows, per_owner, edge * edge * every)
    return pl.pallas_call(
        functools.partial(conv_kernel, (lax.axis_size("grid"), lax.axis_size("pts"))),
        out_shape=jax.ShapeDtypeStruct(local_sums.shape, jnp.bfloat16),
        in_specs=[pl.BlockSpec(memory_space=pltpu.VMEM)] * 8,
        out_specs=pl.BlockSpec(memory_space=pltpu.VMEM),
        scratch_shapes=[
            pltpu.VMEM(sent_ids.shape, jnp.bfloat16),
            pltpu.VMEM(queue, jnp.bfloat16),
            pltpu.VMEM(queue, jnp.bfloat16),
            pltpu.VMEM(queue, jnp.bfloat16),
            pltpu.VMEM(queue, jnp.bfloat16),
            pltpu.VMEM((edge, edge * blocks, every), jnp.float32),
            pltpu.VMEM((layers * 9, every, every), jnp.bfloat16),
            pltpu.VMEM((edge, edge, blocks, every), jnp.bfloat16),
            pltpu.VMEM((edge + 2, edge + 2, blocks, every), jnp.bfloat16),
            pltpu.VMEM(halo, jnp.bfloat16),
            pltpu.VMEM(halo, jnp.bfloat16),
            pltpu.SemaphoreType.DMA(halo[:2]),
            pltpu.SemaphoreType.DMA(halo[:2]),
            pltpu.SemaphoreType.DMA((rows,)),
            pltpu.SemaphoreType.DMA((rows,)),
            pltpu.SemaphoreType.DMA((edge, rows)),
            pltpu.SemaphoreType.DMA((edge, rows)),
            pltpu.SemaphoreType.DMA((edge, rows)),
            pltpu.SemaphoreType.DMA((edge, rows)),
            pltpu.SemaphoreType.DMA((edge + 1,)),
        ],
        compiler_params=pltpu.CompilerParams(collective_id=0, has_side_effects=True),
    )(sent_ids, send_picks, local_sums, stacked, *selectors)


def per_device(
    features, w_in, w_mid, w_conv, point_frac, point_base, slot_dest, slot_tile_block, slot_count
):
    slot_total = slot_dest.shape[0]
    slot_width = features.shape[1] // slot_total
    owners = lax.axis_size("grid")
    per_owner = max(2, 2 * slot_total // owners)
    queue_length = owners * per_owner
    hidden_one = point_layer(w_in, features)
    hidden_two = point_layer(w_mid, hidden_one)
    channels = hidden_two.shape[0]
    hidden_two = hidden_two.reshape(channels, slot_total, slot_width)
    offsets = point_frac.reshape(3, slot_total, slot_width)
    corners = point_base.reshape(3, slot_total, slot_width)
    slot_order = jnp.arange(slot_total, dtype=jnp.int32)
    same_owner = (slot_dest[:, None] == slot_dest[None, :]) & (
        slot_order[None, :] < slot_order[:, None]
    )
    rank_within = jnp.sum(same_owner.astype(jnp.int32), axis=1)
    send_place = slot_dest * per_owner + rank_within
    send_match = send_place[None, :] == jnp.arange(queue_length, dtype=jnp.int32)[:, None]
    sent_block = jnp.sum(jnp.where(send_match, slot_tile_block[None, :] + 1, 0), axis=1) - 1
    send_picks = send_match.astype(jnp.bfloat16)
    weights = trilinear(offsets, corners, slot_count, BLOCK_EDGE_CELLS, GZ)
    local_sums = splat(weights, hidden_two).reshape(slot_total, -1)
    sent_ids = jnp.broadcast_to(sent_block[:, None], (queue_length, ID_LANES)).astype(jnp.bfloat16)
    blocks = exchange_and_convolve(
        sent_ids.reshape(owners, per_owner, ID_LANES), send_picks, local_sums, w_conv
    )
    interp = interpolate(weights, blocks)
    point_out = (hidden_two.astype(jnp.float32) + interp.astype(jnp.float32)).astype(jnp.bfloat16)
    return point_out.reshape(channels, slot_total * slot_width)


def solution(mesh):
    return jax.shard_map(
        per_device,
        mesh=mesh,
        in_specs=(
            P(None, ("pts", "grid")),
            P(),
            P(),
            P(),
            P(None, ("pts", "grid")),
            P(None, ("pts", "grid")),
            P(("pts", "grid")),
            P(("pts", "grid")),
            P(("pts", "grid")),
        ),
        out_specs=P(None, ("pts", "grid")),
        check_vma=False,
    )
```

```python
import functools

import jax
import jax.numpy as jnp
import numpy as np
from jax import lax
from jax.experimental import pallas as pl
from jax.experimental.pallas import tpu as pltpu
from jax.sharding import PartitionSpec as P

GZ = 8
BLOCK_EDGE_CELLS = 4
TX = 32
TY = 32
ID_LANES = 128
MESH = pl.DeviceIdType.MESH
DIRECTIONS = ((1, 0), (-1, 0), (0, 1), (0, -1), (1, 1), (1, -1), (-1, 1), (-1, -1))


def point_layer(weight, inputs):
    mixed_sum = lax.dot_general(
        weight, inputs, (((0,), (0,)), ((), ())), preferred_element_type=jnp.float32
    )
    return jax.nn.silu(mixed_sum).astype(jnp.bfloat16)


def axis_weights(offset, corner, positions):
    positions = positions[:, None, None]
    below_part = jnp.where(positions == corner[None], 1.0 - offset[None], 0.0)
    above_part = jnp.where(positions == corner[None] + 1, offset[None], 0.0)
    return below_part + above_part


def trilinear(offsets, corners, counts, block_edge, grid_depth):
    slot_width = offsets.shape[2]
    live_mask = (jnp.arange(slot_width, dtype=jnp.int32)[None, :] < counts[:, None]).astype(
        jnp.float32
    )
    cells = jnp.arange(block_edge * block_edge, dtype=jnp.int32)
    along_x = axis_weights(offsets[0], corners[0], cells // block_edge)
    along_y = axis_weights(offsets[1], corners[1], cells % block_edge)
    along_z = axis_weights(offsets[2], corners[2], jnp.arange(grid_depth, dtype=jnp.int32))
    corner_weights = (along_x * along_y)[:, None] * along_z[None] * live_mask
    return corner_weights.astype(jnp.bfloat16)


def splat(weights, hidden):
    sums = jnp.einsum("czsp,hsp->sczh", weights, hidden, preferred_element_type=jnp.float32)
    return sums.astype(jnp.bfloat16).reshape(sums.shape[0], sums.shape[1], -1)


def interpolate(weights, blocks):
    cells = blocks.reshape(blocks.shape[0], weights.shape[0], weights.shape[1], -1)
    return jnp.einsum("czsp,sczh->hsp", weights, cells, preferred_element_type=jnp.float32).astype(
        jnp.bfloat16
    )


def build_band(w_ref, band_ref):
    width = w_ref.shape[2]
    depth = band_ref.shape[1] // width

    def one(n, carry):
        band_ref[n] = jnp.zeros(band_ref.shape[1:], band_ref.dtype)
        for b in range(depth):
            low, high = max(b - 1, 0), min(b + 2, depth)
            band_ref[n, low * width : high * width, b * width : (b + 1) * width] = w_ref[
                n, (low - b + 1) * width : (high - b + 1) * width, :
            ]
        return carry

    lax.fori_loop(0, band_ref.shape[0], one, 0)


def halo_selectors():
    edge, nbx, nby = BLOCK_EDGE_CELLS, TX // BLOCK_EDGE_CELLS, TY // BLOCK_EDGE_CELLS
    blocks = nbx * nby
    lane = edge * max(nbx, nby)
    cut_sides = np.zeros((4, lane, edge * blocks), np.float32)
    cut_corners = np.zeros((4, lane, blocks), np.float32)
    for k, (da, db) in enumerate(DIRECTIONS):
        bx, by = (nbx - 1 if da > 0 else 0), (nby - 1 if db > 0 else 0)
        if db == 0:
            for j in range(edge):
                for y in range(nby):
                    cut_sides[k, j * nby + y, j * blocks + bx * nby + y] = 1
        elif da == 0:
            for i in range(edge):
                for x in range(nbx):
                    cut_sides[k, i * nbx + x, i * blocks + x * nby + by] = 1
        else:
            cut_corners[k - 4, :, bx * nby + by] = 1
    put_sides = np.zeros((4, edge, blocks, blocks + lane), np.float32)
    put_corners = np.zeros((4, blocks, blocks + 3 * lane), np.float32)
    for k, (da, db) in enumerate(DIRECTIONS):
        for x in range(nbx):
            for y in range(nby):
                row, sx, sy = x * nby + y, x - da, y - db
                out_x, out_y = not 0 <= sx < nbx, not 0 <= sy < nby
                if da == 0 or db == 0:
                    for phase in range(edge):
                        if out_x:
                            column = blocks + phase * nby + sy
                        elif out_y:
                            column = blocks + phase * nbx + sx
                        else:
                            column = sx * nby + sy
                        put_sides[k, phase, row, column] = 1
                else:
                    i, j = (edge - 1 if da > 0 else 0), (edge - 1 if db > 0 else 0)
                    if out_x and out_y:
                        column = blocks + 2 * lane
                    elif out_x:
                        column = blocks + j * nby + sy
                    elif out_y:
                        column = blocks + lane + i * nbx + sx
                    else:
                        column = sx * nby + sy
                    put_corners[k - 4, row, column] = 1
    return [jnp.asarray(m, jnp.bfloat16) for m in (cut_sides, cut_corners, put_sides, put_corners)]


def select(one_hot, values):
    return jnp.dot(one_hot, values, preferred_element_type=jnp.float32).astype(jnp.bfloat16)


def conv_kernel(
    sizes,
    ids_ref,
    send_picks,
    sums_ref,
    w_ref,
    cut_sides,
    cut_corners,
    put_sides,
    put_corners,
    out_ref,
    ids,
    outgoing,
    arrived,
    values,
    returned,
    totals,
    band_ref,
    phases,
    around,
    leaving,
    landing,
    send_sem,
    recv_sem,
    id_send,
    id_recv,
    go_send,
    go_recv,
    back_send,
    back_recv,
    own_sem,
):
    rows, columns = sizes
    edge, blocks, every = BLOCK_EDGE_CELLS, phases.shape[2], phases.shape[3]
    layers = landing.shape[0]
    me_row, me_column = lax.axis_index("grid"), lax.axis_index("pts")

    def present(da, db):
        row, column = me_row + da, me_column + db
        return (row >= 0) & (row < rows) & (column >= 0) & (column < columns)

    def tell(t):
        owner = lax.rem(me_row + t, rows)
        return pltpu.make_async_remote_copy(
            src_ref=ids_ref.at[owner],
            dst_ref=ids.at[me_row],
            send_sem=id_send.at[t],
            recv_sem=id_recv.at[t],
            device_id=(me_column, owner),
            device_id_type=MESH,
        )

    def go(i, t):
        owner = lax.rem(me_row + t, rows)
        part = pl.ds(i * edge * every, edge * every)
        return pltpu.make_async_remote_copy(
            src_ref=outgoing.at[owner, :, part],
            dst_ref=arrived.at[me_row, :, part],
            send_sem=go_send.at[i, t],
            recv_sem=go_recv.at[i, t],
            device_id=(me_column, owner),
            device_id_type=MESH,
        )

    def back(i, t):
        origin = lax.rem(me_row + t, rows)
        part = pl.ds(i * edge * every, edge * every)
        return pltpu.make_async_remote_copy(
            src_ref=values.at[origin, :, part],
            dst_ref=returned.at[me_row, :, part],
            send_sem=back_send.at[i, t],
            recv_sem=back_recv.at[i, t],
            device_id=(me_column, origin),
            device_id_type=MESH,
        )

    def back_own(i):
        part = pl.ds(i * edge * every, edge * every)
        return pltpu.make_async_copy(
            values.at[me_row, :, part], returned.at[me_row, :, part], own_sem.at[i + 1]
        )

    barrier = pltpu.get_barrier_semaphore()
    for t in range(1, rows):
        pl.semaphore_signal(
            barrier,
            inc=1,
            device_id=(me_column, lax.rem(me_row + t, rows)),
            device_id_type=MESH,
        )
    for da, db in DIRECTIONS:
        if db != 0:

            @pl.when(present(da, db))
            def _():
                pl.semaphore_signal(
                    barrier, inc=1, device_id=(me_column + db, me_row + da), device_id_type=MESH
                )

    tall = 3 - (me_row == 0).astype(jnp.int32) - (me_row == rows - 1).astype(jnp.int32)
    wide = 2 - (me_column == 0).astype(jnp.int32) - (me_column == columns - 1).astype(jnp.int32)
    pl.semaphore_wait(barrier, rows - 1 + tall * wide)

    for t in range(1, rows):
        tell(t).start()
    for i in range(edge):
        for j in range(edge):
            lanes = slice((i * edge + j) * every, (i * edge + j + 1) * every)
            outgoing[:, :, lanes] = select(send_picks[...], sums_ref[:, lanes]).reshape(
                outgoing.shape[0], outgoing.shape[1], every
            )
        for t in range(1, rows):
            go(i, t).start()
    own = pltpu.make_async_copy(outgoing.at[me_row], arrived.at[me_row], own_sem.at[0])
    own.start()
    ids[me_row] = ids_ref[me_row]
    build_band(w_ref, band_ref)

    def inner_terms(layer, source):
        window = around[source + 1, 1 : edge + 1].reshape(edge * blocks, every)
        for shift_x in range(3):
            i = source + 1 - shift_x
            if 0 <= i < edge:
                term = jnp.dot(
                    window,
                    band_ref[layer * 9 + shift_x * 3 + 1],
                    preferred_element_type=jnp.float32,
                )
                if source == max(i - 1, 0):
                    totals[i] = term
                else:
                    totals[i] += term

    own.wait()
    for t in range(1, rows):
        tell(t).wait_recv()
    queue = arrived.shape[0] * arrived.shape[1]
    named = ids[...].reshape(queue, ID_LANES).astype(jnp.float32)[:, :blocks]
    places = lax.broadcasted_iota(jnp.int32, (queue, blocks), 1).astype(jnp.float32)
    picks = jnp.where(named == places, 1.0, 0.0).astype(jnp.bfloat16)
    for i in range(edge):
        for t in range(1, rows):
            go(i, t).wait_recv()
        for j in range(edge):
            cell = i * edge + j
            phases[i, j] = lax.dot_general(
                picks,
                arrived[:, :, cell * every : (cell + 1) * every].reshape(queue, every),
                (((0,), (0,)), ((), ())),
                preferred_element_type=jnp.float32,
            ).astype(jnp.bfloat16)
        around[i + 1, 1 : edge + 1] = phases[i]
        if i < edge - 1:
            inner_terms(0, i)

    for layer in range(layers):

        def copy(k):
            da, db = DIRECTIONS[k]
            return pltpu.make_async_remote_copy(
                src_ref=leaving.at[layer, k],
                dst_ref=landing.at[layer, k],
                send_sem=send_sem.at[layer, k],
                recv_sem=recv_sem.at[layer, k],
                device_id=(me_column + db, me_row + da),
                device_id_type=MESH,
            )

        for k, (da, db) in enumerate(DIRECTIONS):
            i, j = (edge - 1 if da > 0 else 0), (edge - 1 if db > 0 else 0)
            if db == 0:
                source = phases[i].reshape(edge * blocks, every)
            elif da == 0:
                source = phases[:, j].reshape(edge * blocks, every)
            else:
                source = phases[i, j]
            leaving[layer, k] = select(cut_sides[k] if k < 4 else cut_corners[k - 4], source)

            @pl.when(present(da, db))
            def _():
                copy(k).start()

        if layer == 0:
            inner_terms(0, edge - 1)
        else:
            for i in range(edge):
                around[i + 1, 1 : edge + 1] = phases[i]
                inner_terms(layer, i)
        for k, (da, db) in enumerate(DIRECTIONS):

            @pl.when(present(-da, -db))
            def _():
                copy(k).wait_recv()

            @pl.when(jnp.logical_not(present(-da, -db)))
            def _():
                landing[layer, k] = jnp.zeros(landing.shape[2:], landing.dtype)

        for k, (da, db) in enumerate(DIRECTIONS):
            to_x = 0 if da > 0 else edge + 1
            to_y = 0 if db > 0 else edge + 1
            i, j = (edge - 1 if da > 0 else 0), (edge - 1 if db > 0 else 0)
            if db == 0:
                for phase in range(edge):
                    around[to_x, phase + 1] = select(
                        put_sides[k, phase],
                        jnp.concatenate([phases[i, phase], landing[layer, k]], axis=0),
                    )
            elif da == 0:
                for phase in range(edge):
                    around[phase + 1, to_y] = select(
                        put_sides[k, phase],
                        jnp.concatenate([phases[phase, j], landing[layer, k]], axis=0),
                    )
            else:
                side_x = DIRECTIONS.index((da, 0))
                side_y = DIRECTIONS.index((0, db))
                around[to_x, to_y] = select(
                    put_corners[k - 4],
                    jnp.concatenate(
                        [
                            phases[i, j],
                            landing[layer, side_x],
                            landing[layer, side_y],
                            landing[layer, k],
                        ],
                        axis=0,
                    ),
                )

        for i in range(edge):
            total = totals[i]
            for shift_x in range(3):
                for shift_y in range(3):
                    if shift_y == 1 and 1 <= i + shift_x <= edge:
                        continue
                    window = around[i + shift_x, shift_y : shift_y + edge]
                    total = total + jnp.dot(
                        window.reshape(edge * blocks, every),
                        band_ref[layer * 9 + shift_x * 3 + shift_y],
                        preferred_element_type=jnp.float32,
                    )
            activated = (total / (1.0 + jnp.exp(-total))).astype(jnp.bfloat16)
            phases[i] = activated.reshape(edge, blocks, every)
            if layer == layers - 1:
                for j in range(edge):
                    cell = i * edge + j
                    values[:, :, cell * every : (cell + 1) * every] = select(
                        picks, phases[i, j]
                    ).reshape(values.shape[0], values.shape[1], every)
                for t in range(1, rows):
                    back(i, t).start()
                back_own(i).start()

    for t in range(1, rows):
        tell(t).wait_send()
        for i in range(edge):
            go(i, t).wait_send()
    for i in range(edge):
        back_own(i).wait()
        for t in range(1, rows):
            back(i, t).wait_recv()
        for j in range(edge):
            lanes = slice((i * edge + j) * every, (i * edge + j + 1) * every)
            out_ref[:, lanes] = lax.dot_general(
                send_picks[...],
                returned[:, :, lanes].reshape(queue, every),
                (((0,), (0,)), ((), ())),
                preferred_element_type=jnp.float32,
            ).astype(jnp.bfloat16)
    for i in range(edge):
        for t in range(1, rows):
            back(i, t).wait_send()
    for layer in range(layers):
        for k, (da, db) in enumerate(DIRECTIONS):

            @pl.when(present(da, db))
            def _():
                pltpu.make_async_remote_copy(
                    src_ref=leaving.at[layer, k],
                    dst_ref=landing.at[layer, k],
                    send_sem=send_sem.at[layer, k],
                    recv_sem=recv_sem.at[layer, k],
                    device_id=(me_column + db, me_row + da),
                    device_id_type=MESH,
                ).wait_send()


def exchange_and_convolve(sent_ids, send_picks, local_sums, w_conv):
    edge = BLOCK_EDGE_CELLS
    blocks = (TX // edge) * (TY // edge)
    layers, channels, outs = w_conv.shape[0], w_conv.shape[4], w_conv.shape[5]
    every = GZ * channels
    rows, per_owner = sent_ids.shape[:2]
    stacked = w_conv.reshape(layers * 9, 3 * channels, outs)
    selectors = halo_selectors()
    halo = (layers, len(DIRECTIONS), selectors[0].shape[1], every)
    queue = (rows, per_owner, edge * edge * every)
    return pl.pallas_call(
        functools.partial(conv_kernel, (lax.axis_size("grid"), lax.axis_size("pts"))),
        out_shape=jax.ShapeDtypeStruct(local_sums.shape, jnp.bfloat16),
        in_specs=[pl.BlockSpec(memory_space=pltpu.VMEM)] * 8,
        out_specs=pl.BlockSpec(memory_space=pltpu.VMEM),
        scratch_shapes=[
            pltpu.VMEM(sent_ids.shape, jnp.bfloat16),
            pltpu.VMEM(queue, jnp.bfloat16),
            pltpu.VMEM(queue, jnp.bfloat16),
            pltpu.VMEM(queue, jnp.bfloat16),
            pltpu.VMEM(queue, jnp.bfloat16),
            pltpu.VMEM((edge, edge * blocks, every), jnp.float32),
            pltpu.VMEM((layers * 9, every, every), jnp.bfloat16),
            pltpu.VMEM((edge, edge, blocks, every), jnp.bfloat16),
            pltpu.VMEM((edge + 2, edge + 2, blocks, every), jnp.bfloat16),
            pltpu.VMEM(halo, jnp.bfloat16),
            pltpu.VMEM(halo, jnp.bfloat16),
            pltpu.SemaphoreType.DMA(halo[:2]),
            pltpu.SemaphoreType.DMA(halo[:2]),
            pltpu.SemaphoreType.DMA((rows,)),
            pltpu.SemaphoreType.DMA((rows,)),
            pltpu.SemaphoreType.DMA((edge, rows)),
            pltpu.SemaphoreType.DMA((edge, rows)),
            pltpu.SemaphoreType.DMA((edge, rows)),
            pltpu.SemaphoreType.DMA((edge, rows)),
            pltpu.SemaphoreType.DMA((edge + 1,)),
        ],
        compiler_params=pltpu.CompilerParams(collective_id=0, has_side_effects=True),
    )(sent_ids, send_picks, local_sums, stacked, *selectors)


def per_device(
    features, w_in, w_mid, w_conv, point_frac, point_base, slot_dest, slot_tile_block, slot_count
):
    slot_total = slot_dest.shape[0]
    slot_width = features.shape[1] // slot_total
    owners = lax.axis_size("grid")
    per_owner = max(2, 2 * slot_total // owners)
    queue_length = owners * per_owner
    hidden_one = point_layer(w_in, features)
    hidden_two = point_layer(w_mid, hidden_one)
    channels = hidden_two.shape[0]
    hidden_two = hidden_two.reshape(channels, slot_total, slot_width)
    offsets, corners = lax.optimization_barrier(
        (
            point_frac.reshape(3, slot_total, slot_width),
            point_base.reshape(3, slot_total, slot_width),
        )
    )
    slot_order = jnp.arange(slot_total, dtype=jnp.int32)
    same_owner = (slot_dest[:, None] == slot_dest[None, :]) & (
        slot_order[None, :] < slot_order[:, None]
    )
    rank_within = jnp.sum(same_owner.astype(jnp.int32), axis=1)
    send_place = slot_dest * per_owner + rank_within
    send_match = send_place[None, :] == jnp.arange(queue_length, dtype=jnp.int32)[:, None]
    sent_block = jnp.sum(jnp.where(send_match, slot_tile_block[None, :] + 1, 0), axis=1) - 1
    send_picks = send_match.astype(jnp.bfloat16)
    weights = trilinear(offsets, corners, slot_count, BLOCK_EDGE_CELLS, GZ)
    local_sums = splat(weights, hidden_two).reshape(slot_total, -1)
    sent_ids = jnp.broadcast_to(sent_block[:, None], (queue_length, ID_LANES)).astype(jnp.bfloat16)
    blocks = exchange_and_convolve(
        sent_ids.reshape(owners, per_owner, ID_LANES), send_picks, local_sums, w_conv
    )
    interp = interpolate(weights, blocks)
    point_out = (hidden_two.astype(jnp.float32) + interp.astype(jnp.float32)).astype(jnp.bfloat16)
    return point_out.reshape(channels, slot_total * slot_width)


def solution(mesh):
    return jax.shard_map(
        per_device,
        mesh=mesh,
        in_specs=(
            P(None, ("pts", "grid")),
            P(),
            P(),
            P(),
            P(None, ("pts", "grid")),
            P(None, ("pts", "grid")),
            P(("pts", "grid")),
            P(("pts", "grid")),
            P(("pts", "grid")),
        ),
        out_specs=P(None, ("pts", "grid")),
        check_vma=False,
    )
```
